128 devices in a mesh: grp: 4 (over z), term: 32 (over y, x, core).
Axes of the slice: x: 4, y: 4, z: 4, core: 2. Of those that a mesh axis runs over, the one named last changes fastest.
Arguments:
- hidden_states: bfloat16 [65536, 768], P(('grp', 'term')), may hold values from -8 to 8
- lengths: int32 [512], P(('grp', 'term')), may hold values from 32 to 128, as said below
- block_list: int32 [512, 96], P(('grp', 'term')), may hold values from 0 to 128, as said below
- cluster_ids: int32 [512], P(('grp', 'term')), may hold values from 0 to 65535, as said below
- attn_weight: bfloat16 [768, 2304], replicated, may hold values from -4 to 4
- out_weight: bfloat16 [768, 768], replicated, may hold values from -0.21875 to 0.21875
- up_weight: bfloat16 [768, 3072], replicated, may hold values from -0.21875 to 0.21875
- down_weight: bfloat16 [3072, 768], replicated, may hold values from -0.109375 to 0.109375
- head_weight: bfloat16 [768, 768], replicated, may hold values from -0.21875 to 0.21875
- head_gain: float32 [768], replicated, may hold values from 0.1 to 1.9
- vocab_weight: bfloat16 [16384, 768], P('term'), may hold values from -0.21875 to 0.21875
- vocab_bias: bfloat16 [16384], P('term'), may hold values from 0 to 2
- centroids: bfloat16 [65536, 768], P(('grp', 'term')), may hold values from -6 to 6
Outputs:
- sparse_weights: bfloat16 [512, 16384], P('grp', 'term')
- dense_slots: bfloat16 [128, 16, 768], P(('grp', 'term'))
- slot_passage: int32 [128, 16], P(('grp', 'term'))
The draws below stay inside these ranges and needn't reach their ends.
Inputs may be any that keep to these rules, and one draw needn't show every extreme that they name: `lengths`: the first token of every passage is live; some passage has all 128 tokens live. `block_list`: the live entries of a row are distinct term blocks and come first; the rest equal 128, which names no block. Every row has at least 48 live entries and at least one padding entry. The 4 passages of one device have distinct owners (cluster_ids // 512). No owner has more than 16 passages, and some owner has exactly 16.
All inputs are finite; a program needn't handle non-finite values.
Results may differ from the reference program's by a relative error of at most 0.007.
Values may be sent and summed in bfloat16 or wider, within the bound.
No kernel may reach another device: no remote copies, remote signals or barrier semaphores. Data moves between devices by JAX's collectives and lax.ppermute only.
A program may use at most 128 MiB of HBM per device.

```python
import math
import jax
import jax.numpy as jnp
from jax import lax

D = 768
HEAD = 64
FF = 3072
VOCAB = 16384
BLOCK = 128
SEQ = 128
P_DEV = 4
NB = 96
CL_DEV = 512
CAP = 16
PASSAGES = 512
TOKENS = 65536
BLOCKS = 128
CLUSTERS = 65536
DEVICES = 128


def draw_hidden_states(key, part):
    values = jax.random.normal(key, (TOKENS, D), jnp.float32)
    return jnp.clip(values, -8.0, 8.0).astype(jnp.bfloat16)


def draw_attn_weight(key, part):
    values = jax.random.normal(key, (D, 3 * D), jnp.float32) / math.sqrt(D)
    return jnp.clip(values, -4.0, 4.0).astype(jnp.bfloat16)


def draw_lengths(key, part):
    drawn = jax.random.randint(key, (PASSAGES,), SEQ // 4, SEQ + 1)
    places = jnp.arange(PASSAGES, dtype=jnp.int32)
    drawn = jnp.where(places == 0, SEQ, drawn)
    drawn = jnp.where(places == 1, SEQ // 4, drawn)
    return drawn.astype(jnp.int32)


def draw_block_list(key, part):
    row_keys = jax.random.split(key, PASSAGES)
    chosen = jax.vmap(lambda row_key: jax.random.permutation(row_key, BLOCKS)[:NB])(row_keys)
    counts = jax.random.randint(jax.random.fold_in(key, 7), (PASSAGES, 1), NB // 2, NB)
    slots = jnp.arange(NB, dtype=jnp.int32)[None, :]
    return jnp.where(slots < counts, chosen, BLOCKS).astype(jnp.int32)


def draw_cluster_ids(key, part):
    mapping = jax.random.permutation(jax.random.fold_in(key, 31), DEVICES).astype(jnp.int32)
    offsets = jax.random.permutation(jax.random.fold_in(key, 32), DEVICES)[:P_DEV].astype(jnp.int32)
    senders = jnp.arange(DEVICES, dtype=jnp.int32)[:, None]
    owners = mapping[(senders + offsets[None, :]) % DEVICES]
    hottest = jax.random.randint(jax.random.fold_in(key, 33), (), 0, DEVICES).astype(jnp.int32)
    sends_hot = jnp.any(owners == hottest, axis=1)
    priority = jax.random.permutation(jax.random.fold_in(key, 34), DEVICES).astype(jnp.int32)
    score = jnp.where(sends_hot, DEVICES + priority, priority)
    order = jnp.argsort(score, stable=True)
    ranking = jnp.zeros((DEVICES,), jnp.int32).at[order].set(jnp.arange(DEVICES, dtype=jnp.int32))
    extra = ranking < 3 * P_DEV
    owners = owners.at[:, 0].set(jnp.where(extra, hottest, owners[:, 0]))
    within = jax.random.randint(jax.random.fold_in(key, 35), (DEVICES, P_DEV), 0, CL_DEV)
    return (owners * CL_DEV + within).reshape(PASSAGES).astype(jnp.int32)


def block_levels(stream_key, shape, pieces, low, high):
    loudness, own = 1.0, jax.random.fold_in(stream_key, 6)
    for position, parts in pieces:
        draws = jnp.exp(jax.random.uniform(jax.random.fold_in(own, position), (parts,), jnp.float32, low / len(pieces), high / len(pieces)))
        loudness = loudness * jnp.repeat(draws, shape[position] // parts).reshape([-1 if axis == position else 1 for axis in range(len(shape))])
    return loudness


def bell_draw(key, shape, deviation, reach, cuts=(), kind=jnp.bfloat16):
    entries = deviation * jax.random.normal(key, shape, jnp.float32)
    if cuts:
        entries = entries * block_levels(key, shape, cuts, -0.22, 0.18)
    return jnp.clip(entries, -reach, reach).astype(kind)


def setup_inputs(seed: int = 0) -> dict:
    key_of = jax.random.split(jax.random.key(seed), 14)
    hidden_states = draw_hidden_states(jax.random.fold_in(key_of[13], 71), 0)
    lengths = draw_lengths(jax.random.fold_in(key_of[13], 71), 0)
    block_list = draw_block_list(jax.random.fold_in(key_of[13], 71), 0)
    cluster_ids = draw_cluster_ids(jax.random.fold_in(key_of[13], 71), 0)
    attn_weight = draw_attn_weight(jax.random.fold_in(key_of[13], 71), 0)
    out_weight = bell_draw(key_of[5], (D, D), D ** -0.5, 0.21875)
    up_weight = bell_draw(key_of[6], (D, FF), D ** -0.5, 0.21875)
    down_weight = bell_draw(key_of[7], (FF, D), FF ** -0.5, 0.109375)
    head_weight = bell_draw(key_of[8], (D, D), D ** -0.5, 0.21875)
    head_gain = jnp.clip(1.0 + 0.18 * jax.random.normal(key_of[9], (D,), jnp.float32), 0.1, 1.9)
    vocab_weight = bell_draw(key_of[10], (VOCAB, D), D ** -0.5, 0.21875, ((0, 32),))
    vocab_bias = jnp.clip(2.0 * jax.random.uniform(key_of[11], (VOCAB,), jnp.float32) ** block_levels(key_of[11], (VOCAB,), ((0, 32),), -0.2, 0.2), 0.0, 2.0).astype(jnp.bfloat16)
    centroids = bell_draw(key_of[12], (CLUSTERS, D), 1.0, 6.0, ((0, 128),))
    return dict(hidden_states=hidden_states, lengths=lengths, block_list=block_list, cluster_ids=cluster_ids, attn_weight=attn_weight, out_weight=out_weight, up_weight=up_weight, down_weight=down_weight, head_weight=head_weight, head_gain=head_gain, vocab_weight=vocab_weight, vocab_bias=vocab_bias, centroids=centroids)


def layer_norm(values):
    center = values - lax.optimization_barrier(jnp.mean(values, axis=-1, keepdims=True))
    spread = lax.optimization_barrier(jnp.mean(center * center, axis=-1, keepdims=True))
    return center * lax.rsqrt(spread + 1e-06)

def encode(hidden_states, lengths, attn_weight, out_weight, up_weight, down_weight):
    passages = lengths.shape[0]
    seq_len = hidden_states.shape[0] // passages
    width = hidden_states.shape[1]
    head_count = width // HEAD
    joined = jnp.dot(hidden_states, attn_weight, preferred_element_type=jnp.float32).astype(jnp.bfloat16)
    joined = joined.reshape(passages, seq_len, 3, head_count, HEAD).astype(jnp.float32)
    query_heads = joined[:, :, 0]
    key_heads = joined[:, :, 1]
    value_heads = joined[:, :, 2]
    scores = jnp.einsum('pqhd,pkhd->phqk', query_heads, key_heads) / math.sqrt(HEAD)
    live_mask = jnp.arange(seq_len, dtype=jnp.int32)[None, :] < lengths[:, None]
    scores = jnp.where(live_mask[:, None, None, :], scores, -1e+30)
    highest = lax.optimization_barrier(jnp.max(scores, axis=-1, keepdims=True))
    expo = jnp.exp(scores - highest)
    attention = (expo / lax.optimization_barrier(jnp.sum(expo, axis=-1, keepdims=True))).astype(jnp.bfloat16)
    context = jnp.einsum('phqk,pkhd->pqhd', attention.astype(jnp.float32), value_heads)
    context = context.astype(jnp.bfloat16).reshape(passages * seq_len, width)
    mixed = hidden_states.astype(jnp.float32) + jnp.dot(context, out_weight, preferred_element_type=jnp.float32)
    first = layer_norm(mixed).astype(jnp.bfloat16)
    inner = jax.nn.gelu(jnp.dot(first, up_weight, preferred_element_type=jnp.float32), approximate=False).astype(jnp.bfloat16)
    second = first.astype(jnp.float32) + jnp.dot(inner, down_weight, preferred_element_type=jnp.float32)
    return layer_norm(second).astype(jnp.bfloat16)

def head_transform(layer_out, head_weight, head_gain):
    middle = jax.nn.gelu(jnp.dot(layer_out, head_weight, preferred_element_type=jnp.float32), approximate=False)
    return (layer_norm(middle) * head_gain[None, :]).astype(jnp.bfloat16)

def vocab_pool(transformed, lengths, block_list, vocab_weight, vocab_bias, first_col):
    logits = lax.dot_general(transformed, vocab_weight, (((1,), (1,)), ((), ())), preferred_element_type=jnp.float32)
    logits = logits + vocab_bias.astype(jnp.float32)[None, :]
    activity = jnp.log1p(jax.nn.relu(logits))
    passages = lengths.shape[0]
    seq_len = transformed.shape[0] // passages
    columns = vocab_weight.shape[0]
    activity = activity.reshape(passages, seq_len, columns)
    live_mask = (jnp.arange(seq_len, dtype=jnp.int32)[None, :] < lengths[:, None]).astype(jnp.float32)
    pooled = lax.optimization_barrier(jnp.max(activity * live_mask[:, :, None], axis=1))
    block_ids = (first_col + jnp.arange(columns, dtype=jnp.int32)) // BLOCK
    listed = jnp.any(block_list[:, :, None] == block_ids[None, None, :], axis=1)
    return jnp.where(listed, pooled, 0.0).astype(jnp.bfloat16)

def reference(hidden_states, lengths, block_list, cluster_ids, attn_weight, out_weight, up_weight, down_weight, head_weight, head_gain, vocab_weight, vocab_bias, centroids):

    def one_passage(inputs):
        tokens, length_one, listed_one = inputs
        layer_out = encode(tokens, length_one[None], attn_weight, out_weight, up_weight, down_weight)
        transformed = head_transform(layer_out, head_weight, head_gain)
        sparse_row = vocab_pool(transformed, length_one[None], listed_one[None, :], vocab_weight, vocab_bias, jnp.int32(0))
        return (sparse_row[0], layer_out[0])
    sparse_weights, dense_rows = lax.map(one_passage, (hidden_states.reshape(PASSAGES, SEQ, D), lengths, block_list))
    owner_ids = (cluster_ids // CL_DEV).astype(jnp.int32)
    residual = (dense_rows.astype(jnp.float32) - centroids[cluster_ids].astype(jnp.float32)).astype(jnp.bfloat16)
    places = jnp.arange(PASSAGES, dtype=jnp.int32)
    same_owner = owner_ids[:, None] == owner_ids[None, :]
    earlier = places[None, :] < places[:, None]
    ranks = lax.optimization_barrier(jnp.sum((same_owner & earlier).astype(jnp.int32), axis=1)).astype(jnp.int32)
    slot_index = (owner_ids * CAP + ranks).astype(jnp.int32)
    dense_flat = jnp.zeros((DEVICES * CAP, D), jnp.bfloat16).at[slot_index].set(residual)
    passage_flat = jnp.full((DEVICES * CAP,), -1, jnp.int32).at[slot_index].set(places)
    return (sparse_weights, dense_flat.reshape(DEVICES, CAP, D), passage_flat.reshape(DEVICES, CAP))
```

```python
import functools
import math

import jax
import jax.numpy as jnp
from jax import lax
from jax.experimental import pallas as pl
from jax.experimental.pallas import tpu as pltpu
from jax.sharding import PartitionSpec as P

HEAD = 64
BLOCK = 128
SEQ = 128
CL_DEV = 512
CAP = 16
NX = 4
NY = 4
FCH = 512
EXTRA = 16
META = 128
STEP = 256
PARTS = 1
FILL = -1e30
F32 = jnp.float32
BF16 = jnp.bfloat16
I32 = jnp.int32
VMEM_BYTES = 62 * 1024 * 1024

TAIL = (
    -0.9999988675117493,
    -1.151123285293579,
    -0.4591154456138611,
    -0.05271419882774353,
    0.007333385292440653,
    -0.0003233428578823805,
    -0.00011446241842349991,
    2.508325815142598e-05,
    -1.6903979940252611e-06,
)


def vmem():
    return pl.BlockSpec(memory_space=pltpu.VMEM)


def smem():
    return pl.BlockSpec(memory_space=pltpu.SMEM)


def hbm():
    return pl.BlockSpec(memory_space=pltpu.HBM)


def gelu(x):
    mag = jnp.abs(x)
    power = jnp.full_like(mag, TAIL[-1])
    for coefficient in TAIL[-2::-1]:
        power = power * mag + coefficient
    return jnp.maximum(x, 0.0) - mag * jnp.exp2(power)


def normalize(values):
    width = values.shape[-1]
    center = values - jnp.sum(values, axis=-1, keepdims=True) * (1.0 / width)
    spread = jnp.sum(center * center, axis=-1, keepdims=True) * (1.0 / width)
    return center * lax.rsqrt(spread + 1e-06)


def encode_kernel(
    offset,
    lengths_ref, hidden_hbm, lists_ref, gain_ref, attn_hbm, out_hbm, up_hbm, down_hbm, head_hbm,
    send_ref, dense_ref,
    hidden, attn_v, out_v, up_v, down_v, head_v, joined, context, first, acc, sems,
):
    rows, width = hidden.shape
    passages = rows // SEQ
    pairs = width // 128
    chunks = up_v.shape[0]

    moves = [(hidden_hbm.at[pl.ds(offset * SEQ, rows), :], hidden)]
    for k in range(3):
        moves.append((attn_hbm.at[:, pl.ds(k * width, width)], attn_v.at[k]))
    moves.append((out_hbm, out_v))
    for c in range(chunks):
        moves.append((up_hbm.at[:, pl.ds(c * FCH, FCH)], up_v.at[c]))
        moves.append((down_hbm.at[pl.ds(c * FCH, FCH), :], down_v.at[c]))
    moves.append((head_hbm, head_v))
    dma = [pltpu.make_async_copy(s, d, sems.at[i]) for i, (s, d) in enumerate(moves)]
    for d in dma:
        d.start()

    dma[0].wait()
    for k in range(3):
        dma[1 + k].wait()
        joined[:, k * width : (k + 1) * width] = jnp.dot(
            hidden[...], attn_v[k], preferred_element_type=F32
        ).astype(BF16)

    low = lax.broadcasted_iota(I32, (SEQ, 128), 1) < HEAD
    lane = lax.broadcasted_iota(I32, (2 * SEQ, 128), 1)
    ones = jnp.ones((SEQ, 128), BF16)
    scale = math.log2(math.e) / math.sqrt(HEAD)

    @pl.loop(0, passages)
    def _(p):
        at = pl.ds(pl.multiple_of(p * SEQ, SEQ), SEQ)
        length = lengths_ref[offset + p]
        for h in range(pairs):
            q = joined[at, h * 128 : (h + 1) * 128]
            k = joined[at, width + h * 128 : width + (h + 1) * 128]
            v = joined[at, 2 * width + h * 128 : 2 * width + (h + 1) * 128]
            zero = jnp.zeros_like(q)
            both = jnp.concatenate([jnp.where(low, q, zero), jnp.where(low, zero, q)], axis=0)
            s = lax.dot_general(both, k, (((1,), (1,)), ((), ())), preferred_element_type=F32)
            s = jnp.where(lane < length, s, FILL)
            top = jnp.max(s, axis=-1, keepdims=True)
            e = jnp.exp2((s - top) * scale).astype(BF16)
            o = jnp.dot(e, jnp.concatenate([v, ones], axis=1), preferred_element_type=F32)
            num = jnp.where(low, o[:SEQ, :128], o[SEQ:, :128])
            den = jnp.where(low, o[:SEQ, 128:], o[SEQ:, 128:])
            context[at, h * 128 : (h + 1) * 128] = (num / den).astype(BF16)

    dma[4].wait()
    mixed = hidden[...].astype(F32) + jnp.dot(context[...], out_v[...], preferred_element_type=F32)
    first[...] = normalize(mixed).astype(BF16)
    acc[...] = first[...].astype(F32)
    for c in range(chunks):
        dma[5 + 2 * c].wait()
        dma[6 + 2 * c].wait()
        inner = gelu(jnp.dot(first[...], up_v[c], preferred_element_type=F32)).astype(BF16)
        acc[...] += jnp.dot(inner, down_v[c], preferred_element_type=F32)
    layer_out = normalize(acc[...]).astype(BF16)
    first[...] = layer_out
    dma[5 + 2 * chunks].wait()
    middle = gelu(jnp.dot(layer_out, head_v[...], preferred_element_type=F32))
    acc[...] = normalize(middle) * gain_ref[...]

    row = lax.broadcasted_iota(I32, (SEQ, 1), 0)
    slots = lists_ref.shape[1]
    block_id = lax.broadcasted_iota(I32, (BLOCK, slots), 0)
    send_ref[rows:, :] = jnp.zeros((EXTRA, width), BF16)
    for p in range(passages):
        base = p * SEQ
        send_ref[base : base + SEQ, :] = jnp.where(
            row < lengths_ref[offset + p], acc[base : base + SEQ, :], acc[base : base + 1, :]
        ).astype(BF16)
        dense_ref[p : p + 1, :] = first[base : base + 1, :].astype(F32)
        hit = (lists_ref[offset + p : offset + p + 1, :] == block_id).astype(F32).astype(BF16)
        count = lax.dot_general(
            jnp.ones((8, slots), BF16), hit, (((1,), (1,)), ((), ())), preferred_element_type=F32
        )
        send_ref[rows + p : rows + p + 1, 0:BLOCK] = count[0:1, :].astype(BF16)


def encode(part, hidden, lengths, block_list, gain, attn_w, out_w, up_w, down_w, head_w):
    width = hidden.shape[1]
    passages = lengths.shape[0] // PARTS
    rows = passages * SEQ
    ff = up_w.shape[1]
    chunks = ff // FCH
    flops = 2 * rows * width * (3 * width + width + 2 * ff + width)
    return pl.pallas_call(
        functools.partial(encode_kernel, part * passages),
        out_shape=(
            jax.ShapeDtypeStruct((rows + EXTRA, width), BF16),
            jax.ShapeDtypeStruct((8, width), F32),
        ),
        in_specs=[smem(), hbm(), vmem(), vmem(), hbm(), hbm(), hbm(), hbm(), hbm()],
        out_specs=(vmem(), vmem()),
        scratch_shapes=[
            pltpu.VMEM((rows, width), BF16),
            pltpu.VMEM((3, width, width), BF16),
            pltpu.VMEM((width, width), BF16),
            pltpu.VMEM((chunks, width, FCH), BF16),
            pltpu.VMEM((chunks, FCH, width), BF16),
            pltpu.VMEM((width, width), BF16),
            pltpu.VMEM((rows, 3 * width), BF16),
            pltpu.VMEM((rows, width), BF16),
            pltpu.VMEM((rows, width), BF16),
            pltpu.VMEM((rows, width), F32),
            pltpu.SemaphoreType.DMA((6 + 2 * chunks,)),
        ],
        compiler_params=pltpu.CompilerParams(vmem_limit_bytes=VMEM_BYTES),
        cost_estimate=pl.CostEstimate(
            flops=flops, transcendentals=0, bytes_accessed=2 * width * (5 * width + 2 * ff)
        ),
        name="encode",
    )(lengths, hidden, block_list, gain, attn_w, out_w, up_w, down_w, head_w)


def route_kernel(parts, info_ref, *refs):
    dense, out_ref = refs[:parts], refs[parts]
    devices = out_ref.shape[0]
    width = dense[0].shape[1]
    passages = (info_ref.shape[0] - 1) // parts
    row = lax.broadcasted_iota(I32, (devices, 1), 0)
    lane = lax.broadcasted_iota(I32, (devices, META), 1)
    rows = jnp.zeros((devices, width), F32)
    meta = jnp.zeros((devices, META), I32)
    device = info_ref[0]
    for part in range(parts):
        for p in range(passages):
            cluster = info_ref[1 + part * passages + p]
            owner = lax.div(cluster, CL_DEV)
            local = cluster - owner * CL_DEV
            mine = row == owner
            rows = jnp.where(mine, dense[part][p : p + 1, :], rows)
            high = lax.div(local, 256)
            word = jnp.where(lane == 0, 1, 0)
            word = jnp.where(lane == 1, device, word)
            word = jnp.where(lane == 2, part * passages + p, word)
            word = jnp.where(lane == 3, high, word)
            word = jnp.where(lane == 4, local - high * 256, word)
            meta = jnp.where(mine, word, meta)
    out_ref[:, :width] = rows.astype(BF16)
    out_ref[:, width:] = meta.astype(F32).astype(BF16)


def route(device, cluster_ids, dense, devices):
    width = dense[0].shape[1]
    info = jnp.concatenate([device.reshape(1).astype(I32), cluster_ids])
    return pl.pallas_call(
        functools.partial(route_kernel, len(dense)),
        out_shape=jax.ShapeDtypeStruct((devices, width + META), BF16),
        in_specs=[smem()] + [vmem()] * len(dense),
        out_specs=vmem(),
        name="route",
    )(info, *dense)


def place_kernel(passages, recv_ref, cent_ref, dense_ref, slot_ref):
    devices = recv_ref.shape[0]
    width = dense_ref.shape[1]
    meta = recv_ref[:, width:]
    source = lax.broadcasted_iota(I32, (devices, devices), 0)
    other = lax.broadcasted_iota(I32, (devices, devices), 1)
    before = (other < source).astype(F32).astype(BF16)
    rank = jnp.dot(before, meta, preferred_element_type=F32)[:, 0:1]
    valid = meta[:, 0:1].astype(F32)
    slot = lax.broadcasted_iota(I32, (devices, META), 1).astype(F32)
    chosen = ((rank == slot) & (valid > 0.5)).astype(F32).astype(BF16)
    over = (((0,), (0,)), ((), ()))
    picked = lax.dot_general(chosen, recv_ref[...], over, preferred_element_type=F32)[:CAP]
    filled = picked[:, width : width + 1] > 0.5
    local = picked[:, width + 3 : width + 4] * 256.0 + picked[:, width + 4 : width + 5]
    ids = lax.broadcasted_iota(I32, (CAP, cent_ref.shape[0]), 1).astype(F32)
    lookup = ((ids == local) & filled).astype(F32).astype(BF16)
    center = jnp.dot(lookup, cent_ref[...], preferred_element_type=F32)
    dense_ref[...] = jnp.where(filled, picked[:, :width] - center, 0.0).astype(BF16)
    words = lax.dot_general(meta, chosen, over, preferred_element_type=F32)
    ident = words[1:2, :] * passages + words[2:3, :]
    slot_ref[...] = jnp.where(words[0:1, :] > 0.5, ident, -1.0).astype(I32)


def place(recv, centroids, passages):
    width = centroids.shape[1]
    return pl.pallas_call(
        functools.partial(place_kernel, passages),
        out_shape=(
            jax.ShapeDtypeStruct((CAP, width), BF16),
            jax.ShapeDtypeStruct((1, META), I32),
        ),
        in_specs=[vmem(), vmem()],
        out_specs=(vmem(), vmem()),
        name="place",
    )(recv, centroids)


def score_kernel(groups, shards, base_row, info_ref, *refs):
    tokens = refs[: 2 * groups]
    weights = refs[2 * groups : 2 * groups + shards]
    outs = refs[2 * groups + shards : 2 * groups + 2 * shards]
    tok_v, w_v, tok_sem, w_sem = refs[2 * groups + 2 * shards :]
    rows = tok_v.shape[1] - EXTRA
    passages = rows // SEQ
    terms = w_v.shape[1]
    per_device = terms // BLOCK
    tok_dma = [pltpu.make_async_copy(t, tok_v.at[g], tok_sem.at[g]) for g, t in enumerate(tokens)]
    w_dma = [pltpu.make_async_copy(w, w_v.at[s], w_sem.at[s]) for s, w in enumerate(weights)]
    tok_dma[0].start()
    w_dma[0].start()
    for d in tok_dma[1:]:
        d.start()
    for d in w_dma[1:]:
        d.start()
    core = info_ref[shards]
    source = lax.broadcasted_iota(I32, (BLOCK, terms), 0)
    target = lax.div(lax.broadcasted_iota(I32, (BLOCK, terms), 1), BLOCK)
    row = lax.broadcasted_iota(I32, (8, 1), 0)
    for s in range(shards):
        w_dma[s].wait()
        spread = (source == target + info_ref[s] * per_device).astype(F32).astype(BF16)
        for g in range(groups):
            listed = []
            for c in range(2):
                if s == 0:
                    tok_dma[2 * g + c].wait()
                listed.append(
                    jnp.dot(
                        tok_v[2 * g + c, rows:, 0:BLOCK], spread, preferred_element_type=F32
                    )
                )
            for n in range(terms // STEP):
                at = slice(n * STEP, (n + 1) * STEP)
                tile = jnp.full((8, STEP), FILL, F32)
                for c in range(2):
                    logits = lax.dot_general(
                        tok_v[2 * g + c, :rows, :], w_v[s, at, :], (((1,), (1,)), ((), ())),
                        preferred_element_type=F32,
                    )
                    best = jnp.max(logits.reshape(passages, SEQ, STEP), axis=1)
                    best = jnp.where(listed[c][:passages, at] > 0.5, best, FILL)
                    position = core if c == 0 else 1 - core
                    for p in range(passages):
                        tile = jnp.where(
                            row == position * 4 + base_row + p, best[p : p + 1, :], tile
                        )
                outs[s][g, :, at] = tile


def score(part, info, tokens, weights):
    groups, shards = len(tokens) // 2, len(weights)
    rows, width = tokens[0].shape
    terms = weights[0].shape[0]
    passages = (rows - EXTRA) // SEQ
    flops = 2 * 2 * groups * rows * width * terms * shards
    return pl.pallas_call(
        functools.partial(score_kernel, groups, shards, part * passages),
        out_shape=tuple(
            jax.ShapeDtypeStruct((groups, 8, terms), F32) for _ in range(shards)
        ),
        in_specs=[smem()] + [hbm()] * (2 * groups + shards),
        out_specs=(vmem(),) * shards,
        scratch_shapes=[
            pltpu.VMEM((2 * groups, rows, width), BF16),
            pltpu.VMEM((shards, terms, width), BF16),
            pltpu.SemaphoreType.DMA((2 * groups,)),
            pltpu.SemaphoreType.DMA((shards,)),
        ],
        compiler_params=pltpu.CompilerParams(vmem_limit_bytes=VMEM_BYTES),
        cost_estimate=pl.CostEstimate(
            flops=flops, transcendentals=0, bytes_accessed=shards * terms * width * 2
        ),
        name="score",
    )(info, *tokens, *weights)


def finish_kernel(plan, info_ref, bias_ref, *refs):
    pieces, (out_ref, best) = refs[: len(plan)], refs[len(plan) :]
    y, x = info_ref[0], info_ref[1]
    bias = bias_ref[...].astype(F32)
    seen = set()
    for (dx, dys), piece in zip(plan, pieces):
        for g, dy in enumerate(dys):
            spot = lax.rem(y + dy, NY) * NX + lax.rem(x + dx, NX)
            at = pl.ds(pl.multiple_of(spot * 8, 8), 8)
            if (dx, dy) in seen:
                best[at, :] = jnp.maximum(best[at, :], piece[g])
            else:
                best[at, :] = piece[g]
            seen.add((dx, dy))
    out_ref[...] = jnp.log1p(jnp.maximum(best[...] + bias, 0.0)).astype(BF16)


def finish(info, bias, plan, pieces):
    terms = bias.shape[1]
    rows = NX * NY * 8
    return pl.pallas_call(
        functools.partial(finish_kernel, tuple(plan)),
        out_shape=jax.ShapeDtypeStruct((rows, terms), BF16),
        in_specs=[smem()] + [vmem()] * (1 + len(pieces)),
        out_specs=vmem(),
        scratch_shapes=[pltpu.VMEM((rows, terms), F32)],
        name="finish",
    )(info, bias, *pieces)


def shift(value, dy, dx, swap=False):
    pairs = []
    for y in range(NY):
        for x in range(NX):
            for c in range(2):
                source = (((y + dy) % NY) * NX + (x + dx) % NX) * 2 + (c ^ int(swap))
                pairs.append((source, (y * NX + x) * 2 + c))
    return lax.ppermute(value, "term", pairs)


def body(
    hidden_states,
    lengths,
    block_list,
    cluster_ids,
    attn_weight,
    out_weight,
    up_weight,
    down_weight,
    head_weight,
    head_gain,
    vocab_weight,
    vocab_bias,
    centroids,
):
    term = lax.axis_index("term").astype(I32)
    core = lax.rem(term, 2)
    x = lax.rem(lax.div(term, 2), NX)
    y = lax.div(term, 2 * NX)
    devices = lax.axis_size("grp") * lax.axis_size("term")
    device = lax.axis_index("grp").astype(I32) * lax.axis_size("term") + term
    passages = lengths.shape[0]
    offsets = (0, 1, 3, 2)

    shards = [vocab_weight] + [shift(vocab_weight, 0, d) for d in offsets[1:]]
    info = jnp.stack([(y * NX + lax.rem(x + d, NX)) * 2 + core for d in offsets] + [core])
    gain = head_gain.reshape(1, -1)

    pieces, plan, dense = [], [], []
    sent = []
    for part in range(PARTS):
        payload, rows = encode(
            part, hidden_states, lengths, block_list, gain,
            attn_weight, out_weight, up_weight, down_weight, head_weight,
        )
        dense.append(rows)
        sent.append(payload)

    received = []
    for part in range(PARTS):
        mine = [sent[part]] + [shift(sent[part], d, 0) for d in offsets[1:]]
        other = [shift(m, 0, 0, swap=True) for m in mine]
        received.append((mine, other))

    recv = lax.all_to_all(
        route(device, cluster_ids, dense, devices), ("grp", "term"),
        split_axis=0, concat_axis=0, tiled=True,
    )
    dense_part, slot_part = place(recv, centroids, passages)

    for part in range(PARTS):
        mine, other = received[part]
        for which in ((0,), (1, 2), (3,)):
            tokens = [t for k in which for t in (mine[k], other[k])]
            results = score(part, info, tokens, shards)
            dys = tuple(offsets[k] for k in which)
            for k, d in enumerate(offsets):
                plan.append((((NX - d) % NX), dys))
                pieces.append(results[k] if d == 0 else shift(results[k], 0, (NX - d) % NX))

    sparse = finish(jnp.stack([y, x]), vocab_bias.reshape(1, -1), plan, pieces)
    return (sparse, dense_part[None], slot_part[:, :CAP])


def solution(mesh):
    placed = (
        P(("grp", "term"), None),
        P(("grp", "term")),
        P(("grp", "term"), None),
        P(("grp", "term")),
        P(),
        P(),
        P(),
        P(),
        P(),
        P(),
        P("term", None),
        P("term"),
        P(("grp", "term"), None),
    )
    return jax.shard_map(
        body,
        mesh=mesh,
        in_specs=placed,
        out_specs=(P("grp", "term"), P(("grp", "term"), None, None), P(("grp", "term"), None)),
        check_vma=False,
    )
```

```python
import functools
import math

import jax
import jax.numpy as jnp
from jax import lax
from jax.experimental import pallas as pl
from jax.experimental.pallas import tpu as pltpu
from jax.sharding import PartitionSpec as P

HEAD = 64
BLOCK = 128
SEQ = 128
CL_DEV = 512
CAP = 16
NX = 4
NY = 4
FCH = 512
EXTRA = 16
META = 128
STEP = 256
PARTS = 2
OFFSETS = (0, 1, 3, 2)
PEERS = tuple((dx, dc) for dx in OFFSETS for dc in (0, 1))
FILL = -1e30
F32 = jnp.float32
BF16 = jnp.bfloat16
I32 = jnp.int32
VMEM_BYTES = 62 * 1024 * 1024

TAIL = (
    -0.9999988675117493,
    -1.151123285293579,
    -0.4591154456138611,
    -0.05271419882774353,
    0.007333385292440653,
    -0.0003233428578823805,
    -0.00011446241842349991,
    2.508325815142598e-05,
    -1.6903979940252611e-06,
)


def vmem():
    return pl.BlockSpec(memory_space=pltpu.VMEM)


def smem():
    return pl.BlockSpec(memory_space=pltpu.SMEM)


def hbm():
    return pl.BlockSpec(memory_space=pltpu.HBM)


def gelu(x):
    mag = jnp.abs(x)
    power = jnp.full_like(mag, TAIL[-1])
    for coefficient in TAIL[-2::-1]:
        power = power * mag + coefficient
    return jnp.maximum(x, 0.0) - mag * jnp.exp2(power)


def normalize(values):
    width = values.shape[-1]
    center = values - jnp.sum(values, axis=-1, keepdims=True) * (1.0 / width)
    spread = jnp.sum(center * center, axis=-1, keepdims=True) * (1.0 / width)
    return center * lax.rsqrt(spread + 1e-06)


def attend_kernel(
    lengths_ref, hidden_hbm, attn_hbm, out_hbm, first_ref,
    hidden, attn_v, out_v, joined, context, sems,
):
    rows, width = hidden.shape
    passages = rows // SEQ
    pairs = width // 128
    moves = [(hidden_hbm, hidden)]
    for k in range(3):
        moves.append((attn_hbm.at[:, pl.ds(k * width, width)], attn_v.at[k]))
    moves.append((out_hbm, out_v))
    dma = [pltpu.make_async_copy(s, d, sems.at[i]) for i, (s, d) in enumerate(moves)]
    for d in dma:
        d.start()
    dma[0].wait()
    for k in range(3):
        dma[1 + k].wait()
        joined[:, k * width : (k + 1) * width] = jnp.dot(
            hidden[...], attn_v[k], preferred_element_type=F32
        ).astype(BF16)

    low = lax.broadcasted_iota(I32, (SEQ, 128), 1) < HEAD
    lane = lax.broadcasted_iota(I32, (2 * SEQ, 128), 1)
    ones = jnp.ones((SEQ, 128), BF16)
    scale = math.log2(math.e) / math.sqrt(HEAD)

    @pl.loop(0, passages)
    def _(p):
        at = pl.ds(pl.multiple_of(p * SEQ, SEQ), SEQ)
        length = lengths_ref[p]
        for h in range(pairs):
            q = joined[at, h * 128 : (h + 1) * 128]
            k = joined[at, width + h * 128 : width + (h + 1) * 128]
            v = joined[at, 2 * width + h * 128 : 2 * width + (h + 1) * 128]
            zero = jnp.zeros_like(q)
            both = jnp.concatenate([jnp.where(low, q, zero), jnp.where(low, zero, q)], axis=0)
            s = lax.dot_general(both, k, (((1,), (1,)), ((), ())), preferred_element_type=F32)
            s = jnp.where(lane < length, s, FILL)
            top = jnp.max(s, axis=-1, keepdims=True)
            e = jnp.exp2((s - top) * scale).astype(BF16)
            o = jnp.dot(e, jnp.concatenate([v, ones], axis=1), preferred_element_type=F32)
            num = jnp.where(low, o[:SEQ, :128], o[SEQ:, :128])
            den = jnp.where(low, o[:SEQ, 128:], o[SEQ:, 128:])
            context[at, h * 128 : (h + 1) * 128] = (num / den).astype(BF16)

    dma[4].wait()
    mixed = hidden[...].astype(F32) + jnp.dot(context[...], out_v[...], preferred_element_type=F32)
    first_ref[...] = normalize(mixed).astype(BF16)


def attend(hidden, lengths, attn_w, out_w):
    rows, width = hidden.shape
    return pl.pallas_call(
        attend_kernel,
        out_shape=jax.ShapeDtypeStruct((rows, width), BF16),
        in_specs=[smem(), hbm(), hbm(), hbm()],
        out_specs=vmem(),
        scratch_shapes=[
            pltpu.VMEM((rows, width), BF16),
            pltpu.VMEM((3, width, width), BF16),
            pltpu.VMEM((width, width), BF16),
            pltpu.VMEM((rows, 3 * width), BF16),
            pltpu.VMEM((rows, width), BF16),
            pltpu.SemaphoreType.DMA((5,)),
        ],
        compiler_params=pltpu.CompilerParams(vmem_limit_bytes=VMEM_BYTES),
        cost_estimate=pl.CostEstimate(
            flops=2 * rows * width * 4 * width, transcendentals=0, bytes_accessed=8 * width * width
        ),
        name="attend",
    )(lengths, hidden, attn_w, out_w)


def forward_kernel(
    offset,
    lengths_ref, first_hbm, lists_ref, gain_ref, up_hbm, down_hbm, head_hbm,
    send_ref, dense_ref,
    first, up_v, down_v, head_v, wide, acc, sems,
):
    rows, width = first.shape
    passages = rows // SEQ
    chunks = up_v.shape[0]
    moves = [(first_hbm.at[pl.ds(offset * SEQ, rows), :], first)]
    for c in range(chunks):
        moves.append((up_hbm.at[:, pl.ds(c * FCH, FCH)], up_v.at[c]))
    moves.append((down_hbm, down_v))
    moves.append((head_hbm, head_v))
    dma = [pltpu.make_async_copy(s, d, sems.at[i]) for i, (s, d) in enumerate(moves)]
    for d in dma:
        d.start()

    def up(c):
        dma[1 + c].wait()
        return jnp.dot(first[...], up_v[c], preferred_element_type=F32)

    dma[0].wait()
    current = up(0)
    for c in range(chunks):
        following = up(c + 1) if c + 1 < chunks else None
        wide[:, c * FCH : (c + 1) * FCH] = gelu(current).astype(BF16)
        current = following
    dma[1 + chunks].wait()
    second = first[...].astype(F32) + jnp.dot(
        wide[...], down_v[...], preferred_element_type=F32
    )
    layer_out = normalize(second).astype(BF16)
    first[...] = layer_out
    dma[2 + chunks].wait()
    middle = gelu(jnp.dot(layer_out, head_v[...], preferred_element_type=F32))
    acc[...] = normalize(middle) * gain_ref[...].reshape(1, width)

    row = lax.broadcasted_iota(I32, (SEQ, 1), 0)
    slots = lists_ref.shape[1]
    block_id = lax.broadcasted_iota(I32, (BLOCK, slots), 0)
    send_ref[rows:, :] = jnp.zeros((EXTRA, width), BF16)
    for p in range(passages):
        base = p * SEQ
        send_ref[base : base + SEQ, :] = jnp.where(
            row < lengths_ref[offset + p], acc[base : base + SEQ, :], acc[base : base + 1, :]
        ).astype(BF16)
        dense_ref[p : p + 1, :] = first[base : base + 1, :].astype(F32)
        hit = (lists_ref[offset + p : offset + p + 1, :] == block_id).astype(F32).astype(BF16)
        count = lax.dot_general(
            jnp.ones((8, slots), BF16), hit, (((1,), (1,)), ((), ())), preferred_element_type=F32
        )
        send_ref[rows + p : rows + p + 1, 0:BLOCK] = count[0:1, :].astype(BF16)


def forward(part, first, lengths, block_list, gain, up_w, down_w, head_w):
    width = first.shape[1]
    passages = lengths.shape[0] // PARTS
    rows = passages * SEQ
    ff = up_w.shape[1]
    chunks = ff // FCH
    return pl.pallas_call(
        functools.partial(forward_kernel, part * passages),
        out_shape=(
            jax.ShapeDtypeStruct((rows + EXTRA, width), BF16),
            jax.ShapeDtypeStruct((8, width), F32),
        ),
        in_specs=[smem(), hbm(), vmem(), vmem(), hbm(), hbm(), hbm()],
        out_specs=(vmem(), vmem()),
        scratch_shapes=[
            pltpu.VMEM((rows, width), BF16),
            pltpu.VMEM((chunks, width, FCH), BF16),
            pltpu.VMEM((ff, width), BF16),
            pltpu.VMEM((width, width), BF16),
            pltpu.VMEM((rows, ff), BF16),
            pltpu.VMEM((rows, width), F32),
            pltpu.SemaphoreType.DMA((3 + chunks,)),
        ],
        compiler_params=pltpu.CompilerParams(vmem_limit_bytes=VMEM_BYTES),
        cost_estimate=pl.CostEstimate(flops=1, transcendentals=0, bytes_accessed=1),
        name="forward",
    )(lengths, first, block_list, gain, up_w, down_w, head_w)


def here():
    term = lax.axis_index("term").astype(I32)
    chip = lax.div(term, 2)
    return lax.div(chip, NX), lax.rem(chip, NX), lax.rem(term, 2)


def route_kernel(parts, clusters_ref, *refs):
    dense, out_ref = refs[:parts], refs[parts]
    devices = out_ref.shape[0]
    pieces = dense[0].shape[1] // META
    passages = clusters_ref.shape[0] // parts
    row = lax.broadcasted_iota(I32, (devices, 1), 0)
    lane = lax.broadcasted_iota(I32, (devices, META), 1)
    term = lax.axis_index("term").astype(I32)
    device = lax.axis_index("grp").astype(I32) * lax.axis_size("term") + term
    rows = [jnp.zeros((devices, META), F32) for _ in range(pieces)]
    meta = jnp.zeros((devices, META), I32)
    for part in range(parts):
        for p in range(passages):
            cluster = clusters_ref[part * passages + p]
            owner = lax.div(cluster, CL_DEV)
            mine = row == owner
            for k in range(pieces):
                piece = dense[part][p : p + 1, k * META : (k + 1) * META]
                rows[k] = jnp.where(mine, piece, rows[k])
            word = jnp.where(lane == 0, 1, 0)
            word = jnp.where(lane == 1, device, word)
            word = jnp.where(lane == 2, part * passages + p, word)
            word = jnp.where(lane == 3, cluster - owner * CL_DEV, word)
            meta = jnp.where(mine, word, meta)
    for k in range(pieces):
        out_ref[:, k, :] = rows[k]
    out_ref[:, pieces, :] = meta.astype(F32)
    out_ref[:, pieces + 1, :] = jnp.zeros((devices, META), F32)


def route(cluster_ids, dense, devices):
    return pl.pallas_call(
        functools.partial(route_kernel, len(dense)),
        out_shape=jax.ShapeDtypeStruct((devices, 8, META), F32),
        in_specs=[smem()] + [vmem()] * len(dense),
        out_specs=vmem(),
        cost_estimate=pl.CostEstimate(flops=1, transcendentals=0, bytes_accessed=1),
        name="route",
    )(cluster_ids, *dense)


def place_kernel(passages, recv_ref, cent_ref, dense_ref, slot_ref):
    devices = recv_ref.shape[0]
    width = dense_ref.shape[1]
    pieces = width // META
    words = recv_ref[:, pieces, :]
    high = jnp.floor(words * (1.0 / 256.0))
    meta = words.astype(BF16)
    source = lax.broadcasted_iota(I32, (devices, devices), 0)
    other = lax.broadcasted_iota(I32, (devices, devices), 1)
    before = (other < source).astype(F32).astype(BF16)
    valid = words[:, 0:1]
    rank = jnp.dot(before, meta, preferred_element_type=F32)[:, 0:1]
    slot = lax.broadcasted_iota(I32, (devices, META), 1).astype(F32)
    chosen = ((rank == slot) & (valid > 0.5)).astype(F32).astype(BF16)
    over = (((0,), (0,)), ((), ()))

    def pick(values):
        return lax.dot_general(
            chosen, values.astype(BF16), over, preferred_element_type=F32
        )[:CAP]

    small = pick(words - high * 256.0)
    large = pick(high)
    filled = small[:, 0:1] > 0.5
    local = (small + large * 256.0)[:, 3:4]
    ids = lax.broadcasted_iota(I32, (CAP, cent_ref.shape[0]), 1).astype(F32)
    lookup = ((ids == local) & filled).astype(F32).astype(BF16)
    center = jnp.dot(lookup, cent_ref[...], preferred_element_type=F32)
    for k in range(pieces):
        at = slice(k * META, (k + 1) * META)
        dense_ref[:, at] = jnp.where(
            filled, pick(recv_ref[:, k, :]) - center[:, at], 0.0
        ).astype(BF16)
    names = lax.dot_general(meta, chosen, over, preferred_element_type=F32)
    ident = names[1:2, :] * passages + names[2:3, :]
    slot_ref[...] = jnp.where(names[0:1, :] > 0.5, ident, -1.0).astype(I32)


def place(recv, centroids, passages):
    width = centroids.shape[1]
    return pl.pallas_call(
        functools.partial(place_kernel, passages),
        out_shape=(
            jax.ShapeDtypeStruct((CAP, width), BF16),
            jax.ShapeDtypeStruct((1, META), I32),
        ),
        in_specs=[vmem(), vmem()],
        out_specs=(vmem(), vmem()),
        name="place",
    )(recv, centroids)


def score_kernel(base_row, tokens, vocab_hbm, earlier, res, outs, tok_v, side_v, w_v, tok_sem, side_sem, w_sem):
    groups, rows, width = tok_v.shape
    passages = rows // SEQ
    shards, terms = w_v.shape[:2]
    per_device = terms // BLOCK
    span = 2 * rows
    tok_dma, side_dma, w_dma = [], [], []
    for g, t in enumerate(tokens):
        tok_dma.append(
            pltpu.make_async_copy(t.at[pl.ds(0, rows), :], tok_v.at[g], tok_sem.at[g])
        )
        side_dma.append(
            pltpu.make_async_copy(
                t.at[pl.ds(rows, EXTRA), pl.ds(0, BLOCK)], side_v.at[g], side_sem.at[g]
            )
        )
    for s in range(shards):
        w_dma.append(
            pltpu.make_async_copy(
                vocab_hbm.at[pl.ds(s * terms, terms), :], w_v.at[s], w_sem.at[s]
            )
        )
    for d in tok_dma[:2] + w_dma[:1] + tok_dma[2:] + side_dma + w_dma[1:]:
        d.start()
    y, x, core = here()
    source = lax.broadcasted_iota(I32, (BLOCK, terms), 0)
    target = lax.div(lax.broadcasted_iota(I32, (BLOCK, terms), 1), BLOCK)
    row = lax.broadcasted_iota(I32, (8, 1), 0)
    for d in tok_dma + side_dma:
        d.wait()

    @pl.loop(0, shards)
    def _(s):
        pltpu.make_async_copy(
            vocab_hbm.at[pl.ds(pl.multiple_of(s * terms, terms), terms), :], w_v.at[s], w_sem.at[s]
        ).wait()
        owner = y * (2 * NX) + s
        spread = (source == target + owner * per_device).astype(F32).astype(BF16)
        for j in range(groups // 2):
            listed = [
                jnp.dot(side_v[2 * j + k], spread, preferred_element_type=F32) for k in range(2)
            ]
            both = tok_v[2 * j : 2 * j + 2].reshape(span, width)
            for n in range(terms // STEP):
                at = slice(n * STEP, (n + 1) * STEP)
                logits = lax.dot_general(
                    both, w_v[s, at, :], (((1,), (1,)), ((), ())), preferred_element_type=F32
                )
                best = jnp.max(logits.reshape(2 * passages, SEQ, STEP), axis=1)
                if earlier is None:
                    tile = jnp.full((8, STEP), FILL, F32)
                else:
                    tile = earlier[s, 8 * j : 8 * j + 8, at]
                for g in range(2):
                    for p in range(passages):
                        k = g * passages + p
                        value = jnp.where(
                            listed[g][p : p + 1, at] > 0.5, best[k : k + 1, :], FILL
                        )
                        tile = jnp.where(row == g * 4 + base_row + p, value, tile)
                res[s, 8 * j : 8 * j + 8, at] = tile

    for k, (dx, dc) in enumerate(PEERS if outs else ()):
        spot = lax.rem(x + dx, NX) * 2 + lax.rem(core + dc, 2)
        outs[k][...] = res[spot]


def score(part, tokens, vocab, earlier):
    groups = len(tokens)
    rows, width = tokens[0].shape
    rows -= EXTRA
    shards = 2 * NX
    terms = vocab.shape[0] // shards
    passages = rows // SEQ
    whole = jax.ShapeDtypeStruct((shards, groups * 4, terms), F32)
    last = earlier is not None

    def kernel(*refs):
        refs = list(refs)
        toks, refs = refs[:groups], refs[groups:]
        voc = refs.pop(0)
        before = refs.pop(0) if last else None
        if last:
            outs, refs = refs[:shards], refs[shards:]
            res = refs.pop(0)
        else:
            outs, res = None, refs.pop(0)
        score_kernel(part * passages, toks, voc, before, res, outs, *refs)

    flops = 2 * groups * rows * width * terms * shards
    piece = jax.ShapeDtypeStruct((groups * 4, terms), F32)
    return pl.pallas_call(
        kernel,
        out_shape=(piece,) * shards if last else whole,
        in_specs=[hbm()] * (groups + 1) + [vmem()] * last,
        out_specs=(vmem(),) * shards if last else vmem(),
        scratch_shapes=[pltpu.VMEM(whole.shape, F32)] * last + [
            pltpu.VMEM((groups, rows, width), BF16),
            pltpu.VMEM((groups, EXTRA, BLOCK), BF16),
            pltpu.VMEM((shards, terms, width), BF16),
            pltpu.SemaphoreType.DMA((groups,)),
            pltpu.SemaphoreType.DMA((groups,)),
            pltpu.SemaphoreType.DMA((shards,)),
        ],
        compiler_params=pltpu.CompilerParams(vmem_limit_bytes=VMEM_BYTES),
        cost_estimate=pl.CostEstimate(
            flops=flops, transcendentals=0, bytes_accessed=shards * terms * width * 2
        ),
        name="score",
    )(*tokens, vocab, *((earlier,) if last else ()))


def finish_kernel(bias_ref, *refs):
    pieces, (out_ref, best) = refs[: len(PEERS)], refs[len(PEERS) :]
    y, x, core = here()
    bias = bias_ref[...].astype(F32).reshape(1, -1)
    for k in range(0, len(PEERS), 2):
        dx = PEERS[k][0]
        for g, dy in enumerate(OFFSETS):
            same = pieces[k][4 * g : 4 * g + 4, :]
            other = pieces[k + 1][4 * g : 4 * g + 4, :]
            tile = jnp.where(
                core == 0,
                jnp.concatenate([same, other], axis=0),
                jnp.concatenate([other, same], axis=0),
            )
            spot = lax.rem(y + dy, NY) * NX + lax.rem(x + dx, NX)
            best[pl.ds(pl.multiple_of(spot * 8, 8), 8), :] = tile
    out_ref[...] = jnp.log1p(jnp.maximum(best[...] + bias, 0.0)).astype(BF16)


def finish(bias, pieces):
    terms = bias.shape[0]
    rows = NX * NY * 8
    return pl.pallas_call(
        finish_kernel,
        out_shape=jax.ShapeDtypeStruct((rows, terms), BF16),
        in_specs=[vmem()] * (1 + len(pieces)),
        out_specs=vmem(),
        scratch_shapes=[pltpu.VMEM((rows, terms), F32)],
        name="finish",
    )(bias, *pieces)


def shift(value, dy, dx, dc):
    pairs = []
    for y in range(NY):
        for x in range(NX):
            for c in range(2):
                source = (((y + dy) % NY) * NX + (x + dx) % NX) * 2 + (c ^ dc)
                pairs.append((source, (y * NX + x) * 2 + c))
    return lax.ppermute(value, "term", pairs)


def body(
    hidden_states,
    lengths,
    block_list,
    cluster_ids,
    attn_weight,
    out_weight,
    up_weight,
    down_weight,
    head_weight,
    head_gain,
    vocab_weight,
    vocab_bias,
    centroids,
):
    devices = lax.axis_size("grp") * lax.axis_size("term")
    passages = lengths.shape[0]

    side = 2 * NX
    rows_of_chips = [[g * side + k for k in range(side)] for g in range(NY)]
    vocab = lax.all_gather(
        vocab_weight, "term", axis=0, tiled=True, axis_index_groups=rows_of_chips
    )
    first = attend(hidden_states, lengths, attn_weight, out_weight)
    dense, received = [], []
    for part in range(PARTS):
        payload, rows = forward(
            part, first, lengths, block_list, head_gain, up_weight, down_weight, head_weight
        )
        dense.append(rows)
        received.append([payload] + [shift(payload, d, 0, 0) for d in OFFSETS[1:]])

    recv = lax.all_to_all(
        route(cluster_ids, dense, devices), ("grp", "term"), split_axis=0, concat_axis=0, tiled=True
    )


    scored = score(0, received[0], vocab, None)
    sent = score(1, received[1], vocab, scored)
    pieces = []
    for dx, dc in PEERS:
        back = sent[PEERS.index(((NX - dx) % NX, dc))]
        pieces.append(back if (dx, dc) == (0, 0) else shift(back, 0, dx, dc))
    sparse = finish(vocab_bias, pieces)
    dense_part, slot_part = place(recv, centroids, passages)
    return (sparse, dense_part[None], slot_part[:, :CAP])


def solution(mesh):
    placed = (
        P(("grp", "term"), None),
        P(("grp", "term")),
        P(("grp", "term"), None),
        P(("grp", "term")),
        P(),
        P(),
        P(),
        P(),
        P(),
        P(),
        P("term", None),
        P("term"),
        P(("grp", "term"), None),
    )
    return jax.shard_map(
        body,
        mesh=mesh,
        in_specs=placed,
        out_specs=(P("grp", "term"), P(("grp", "term"), None, None), P(("grp", "term"), None)),
        check_vma=False,
    )
```

```python
import functools
import math

import jax
import jax.numpy as jnp
from jax import lax
from jax.experimental import pallas as pl
from jax.experimental.pallas import tpu as pltpu
from jax.sharding import PartitionSpec as P

HEAD = 64
BLOCK = 128
SEQ = 128
CL_DEV = 512
CAP = 16
NX = 4
NY = 4
FCH = 512
EXTRA = 16
META = 128
STEP = 256
GROUP = 4
PARTS = 2
OFFSETS = (0, 1, 3, 2)
PEERS = tuple((dx, dc) for dx in OFFSETS for dc in (0, 1))
FILL = -1e30
F32 = jnp.float32
BF16 = jnp.bfloat16
I32 = jnp.int32
VMEM_BYTES = 62 * 1024 * 1024

TAIL = (
    -0.9999988675117493,
    -1.151123285293579,
    -0.4591154456138611,
    -0.05271419882774353,
    0.007333385292440653,
    -0.0003233428578823805,
    -0.00011446241842349991,
    2.508325815142598e-05,
    -1.6903979940252611e-06,
)


def vmem():
    return pl.BlockSpec(memory_space=pltpu.VMEM)


def smem():
    return pl.BlockSpec(memory_space=pltpu.SMEM)


def hbm():
    return pl.BlockSpec(memory_space=pltpu.HBM)


def gelu(x):
    mag = jnp.abs(x)
    power = jnp.full_like(mag, TAIL[-1])
    for coefficient in TAIL[-2::-1]:
        power = power * mag + coefficient
    return jnp.maximum(x, 0.0) - mag * jnp.exp2(power)


def normalize(values):
    width = values.shape[-1]
    center = values - jnp.sum(values, axis=-1, keepdims=True) * (1.0 / width)
    spread = jnp.sum(center * center, axis=-1, keepdims=True) * (1.0 / width)
    return center * lax.rsqrt(spread + 1e-06)


def attend_kernel(
    lengths_ref, hidden_hbm, attn_hbm, out_hbm, first_ref,
    hidden, attn_v, out_v, joined, context, sems,
):
    rows, width = hidden.shape
    passages = rows // SEQ
    pairs = width // 128
    moves = [(hidden_hbm, hidden)]
    for k in range(3):
        moves.append((attn_hbm.at[:, pl.ds(k * width, width)], attn_v.at[k]))
    moves.append((out_hbm, out_v))
    dma = [pltpu.make_async_copy(s, d, sems.at[i]) for i, (s, d) in enumerate(moves)]
    for d in dma:
        d.start()
    dma[0].wait()
    dma[1].wait()
    for k in range(3):
        if k == 1:
            for d in dma[2:]:
                d.wait()
        joined[:, k * width : (k + 1) * width] = jnp.dot(
            hidden[...], attn_v[k], preferred_element_type=F32
        ).astype(BF16)

    low = lax.broadcasted_iota(I32, (SEQ, 128), 1) < HEAD
    lane = lax.broadcasted_iota(I32, (2 * SEQ, 128), 1)
    scale = math.log2(math.e) / math.sqrt(HEAD)

    for p in range(passages):
        at = slice(p * SEQ, (p + 1) * SEQ)
        length = lengths_ref[p]
        for h in range(pairs):
            q = joined[at, h * 128 : (h + 1) * 128]
            k = joined[at, width + h * 128 : width + (h + 1) * 128]
            v = joined[at, 2 * width + h * 128 : 2 * width + (h + 1) * 128]
            zero = jnp.zeros_like(q)
            both = jnp.concatenate([jnp.where(low, q, zero), jnp.where(low, zero, q)], axis=0)
            s = lax.dot_general(both, k, (((1,), (1,)), ((), ())), preferred_element_type=F32)
            s = jnp.where(lane < length, s, FILL)
            top = jnp.max(s, axis=-1, keepdims=True)
            e = jnp.exp2((s - top) * scale)
            total = 1.0 / jnp.sum(e, axis=-1, keepdims=True)
            o = jnp.dot(e.astype(BF16), v, preferred_element_type=F32)
            mix = jnp.where(low, o[:SEQ] * total[:SEQ], o[SEQ:] * total[SEQ:])
            context[at, h * 128 : (h + 1) * 128] = mix.astype(BF16)

    for p in range(passages):
        at = slice(p * SEQ, (p + 1) * SEQ)
        mixed = hidden[at, :].astype(F32) + jnp.dot(
            context[at, :], out_v[...], preferred_element_type=F32
        )
        first_ref[at, :] = normalize(mixed).astype(BF16)


def attend(hidden, lengths, attn_w, out_w):
    rows, width = hidden.shape
    return pl.pallas_call(
        attend_kernel,
        out_shape=jax.ShapeDtypeStruct((rows, width), BF16),
        in_specs=[smem(), hbm(), hbm(), hbm()],
        out_specs=vmem(),
        scratch_shapes=[
            pltpu.VMEM((rows, width), BF16),
            pltpu.VMEM((3, width, width), BF16),
            pltpu.VMEM((width, width), BF16),
            pltpu.VMEM((rows, 3 * width), BF16),
            pltpu.VMEM((rows, width), BF16),
            pltpu.SemaphoreType.DMA((5,)),
        ],
        compiler_params=pltpu.CompilerParams(vmem_limit_bytes=VMEM_BYTES),
        cost_estimate=pl.CostEstimate(
            flops=2 * rows * width * 4 * width, transcendentals=0, bytes_accessed=8 * width * width
        ),
        name="attend",
    )(lengths, hidden, attn_w, out_w)


def forward_kernel(
    offset,
    lengths_ref, first_hbm, lists_ref, gain_ref, up_hbm, down_hbm, head_hbm,
    send_ref, dense_ref,
    first, up_v, down_v, head_v, wide, acc, sems,
):
    rows, width = first.shape
    passages = rows // SEQ
    chunks = up_v.shape[0]
    half = chunks // 2
    moves = [(first_hbm.at[pl.ds(offset * SEQ, rows), :], first)]
    for c in range(chunks):
        moves.append((up_hbm.at[:, pl.ds(c * FCH, FCH)], up_v.at[c]))
    moves.append((down_hbm, down_v))
    moves.append((head_hbm, head_v))
    dma = [pltpu.make_async_copy(s, d, sems.at[i]) for i, (s, d) in enumerate(moves)]
    for d in dma:
        d.start()

    def up(c):
        return jnp.dot(first[...], up_v[c], preferred_element_type=F32)

    for part in (0, half):
        for d in dma[1 + part : 1 + part + half] + (dma[:1] if part == 0 else dma[1 + chunks :]):
            d.wait()
        current = up(part)
        for c in range(part, part + half):
            following = up(c + 1) if c + 1 < part + half else None
            wide[:, c * FCH : (c + 1) * FCH] = gelu(current).astype(BF16)
            current = following
    second = first[...].astype(F32) + jnp.dot(
        wide[...], down_v[...], preferred_element_type=F32
    )
    layer_out = normalize(second).astype(BF16)
    first[...] = layer_out
    middle = gelu(jnp.dot(layer_out, head_v[...], preferred_element_type=F32))
    acc[...] = normalize(middle) * gain_ref[...].reshape(1, width)

    row = lax.broadcasted_iota(I32, (SEQ, 1), 0)
    slots = lists_ref.shape[1]
    block_id = lax.broadcasted_iota(I32, (BLOCK, slots), 0)
    send_ref[rows:, :] = jnp.zeros((EXTRA, width), BF16)
    for p in range(passages):
        base = p * SEQ
        send_ref[base : base + SEQ, :] = jnp.where(
            row < lengths_ref[offset + p], acc[base : base + SEQ, :], acc[base : base + 1, :]
        ).astype(BF16)
        dense_ref[p : p + 1, :] = first[base : base + 1, :].astype(F32)
        hit = (lists_ref[offset + p : offset + p + 1, :] == block_id).astype(F32).astype(BF16)
        count = lax.dot_general(
            jnp.ones((8, slots), BF16), hit, (((1,), (1,)), ((), ())), preferred_element_type=F32
        )
        send_ref[rows + p : rows + p + 1, 0:BLOCK] = count[0:1, :].astype(BF16)


def forward(part, first, lengths, block_list, gain, up_w, down_w, head_w):
    width = first.shape[1]
    passages = lengths.shape[0] // PARTS
    rows = passages * SEQ
    ff = up_w.shape[1]
    chunks = ff // FCH
    return pl.pallas_call(
        functools.partial(forward_kernel, part * passages),
        out_shape=(
            jax.ShapeDtypeStruct((rows + EXTRA, width), BF16),
            jax.ShapeDtypeStruct((8, width), F32),
        ),
        in_specs=[smem(), hbm(), vmem(), vmem(), hbm(), hbm(), hbm()],
        out_specs=(vmem(), vmem()),
        scratch_shapes=[
            pltpu.VMEM((rows, width), BF16),
            pltpu.VMEM((chunks, width, FCH), BF16),
            pltpu.VMEM((ff, width), BF16),
            pltpu.VMEM((width, width), BF16),
            pltpu.VMEM((rows, ff), BF16),
            pltpu.VMEM((rows, width), F32),
            pltpu.SemaphoreType.DMA((3 + chunks,)),
        ],
        compiler_params=pltpu.CompilerParams(vmem_limit_bytes=VMEM_BYTES),
        cost_estimate=pl.CostEstimate(flops=1, transcendentals=0, bytes_accessed=1),
        name="forward",
    )(lengths, first, block_list, gain, up_w, down_w, head_w)


def here():
    term = lax.axis_index("term").astype(I32)
    chip = lax.div(term, 2)
    return lax.div(chip, NX), lax.rem(chip, NX), lax.rem(term, 2)


def route_kernel(parts, clusters_ref, *refs):
    dense, out_ref = refs[:parts], refs[parts]
    devices = out_ref.shape[0]
    pieces = dense[0].shape[1] // META
    passages = clusters_ref.shape[0] // parts
    row = lax.broadcasted_iota(I32, (devices, 1), 0)
    lane = lax.broadcasted_iota(I32, (devices, META), 1)
    term = lax.axis_index("term").astype(I32)
    device = lax.axis_index("grp").astype(I32) * lax.axis_size("term") + term
    rows = [jnp.zeros((devices, META), F32) for _ in range(pieces)]
    meta = jnp.zeros((devices, META), I32)
    for part in range(parts):
        for p in range(passages):
            cluster = clusters_ref[part * passages + p]
            owner = lax.div(cluster, CL_DEV)
            mine = row == owner
            for k in range(pieces):
                piece = dense[part][p : p + 1, k * META : (k + 1) * META]
                rows[k] = jnp.where(mine, piece, rows[k])
            word = jnp.where(lane == 0, 1, 0)
            word = jnp.where(lane == 1, device, word)
            word = jnp.where(lane == 2, part * passages + p, word)
            word = jnp.where(lane == 3, cluster - owner * CL_DEV, word)
            meta = jnp.where(mine, word, meta)
    for k in range(pieces):
        out_ref[:, k, :] = rows[k]
    out_ref[:, pieces, :] = meta.astype(F32)
    out_ref[:, pieces + 1, :] = jnp.zeros((devices, META), F32)


def route(cluster_ids, dense, devices):
    return pl.pallas_call(
        functools.partial(route_kernel, len(dense)),
        out_shape=jax.ShapeDtypeStruct((devices, 8, META), F32),
        in_specs=[smem()] + [vmem()] * len(dense),
        out_specs=vmem(),
        cost_estimate=pl.CostEstimate(flops=1, transcendentals=0, bytes_accessed=1),
        name="route",
    )(cluster_ids, *dense)


def place_kernel(passages, recv_ref, cent_ref, dense_ref, slot_ref):
    devices = recv_ref.shape[0]
    width = dense_ref.shape[1]
    pieces = width // META
    words = recv_ref[:, pieces, :]
    high = jnp.floor(words * (1.0 / 256.0))
    meta = words.astype(BF16)
    source = lax.broadcasted_iota(I32, (devices, devices), 0)
    other = lax.broadcasted_iota(I32, (devices, devices), 1)
    before = (other < source).astype(F32).astype(BF16)
    valid = words[:, 0:1]
    rank = jnp.dot(before, meta, preferred_element_type=F32)[:, 0:1]
    slot = lax.broadcasted_iota(I32, (devices, META), 1).astype(F32)
    chosen = ((rank == slot) & (valid > 0.5)).astype(F32).astype(BF16)
    over = (((0,), (0,)), ((), ()))

    def pick(values):
        return lax.dot_general(
            chosen, values.astype(BF16), over, preferred_element_type=F32
        )[:CAP]

    small = pick(words - high * 256.0)
    large = pick(high)
    filled = small[:, 0:1] > 0.5
    local = (small + large * 256.0)[:, 3:4]
    ids = lax.broadcasted_iota(I32, (CAP, cent_ref.shape[0]), 1).astype(F32)
    lookup = ((ids == local) & filled).astype(F32).astype(BF16)
    center = jnp.dot(lookup, cent_ref[...], preferred_element_type=F32)
    for k in range(pieces):
        at = slice(k * META, (k + 1) * META)
        dense_ref[:, at] = jnp.where(
            filled, pick(recv_ref[:, k, :]) - center[:, at], 0.0
        ).astype(BF16)
    names = lax.dot_general(meta, chosen, over, preferred_element_type=F32)
    ident = names[1:2, :] * passages + names[2:3, :]
    slot_ref[...] = jnp.where(names[0:1, :] > 0.5, ident, -1.0).astype(I32)


def place(recv, centroids, passages):
    width = centroids.shape[1]
    return pl.pallas_call(
        functools.partial(place_kernel, passages),
        out_shape=(
            jax.ShapeDtypeStruct((CAP, width), BF16),
            jax.ShapeDtypeStruct((1, META), I32),
        ),
        in_specs=[vmem(), vmem()],
        out_specs=(vmem(), vmem()),
        name="place",
    )(recv, centroids)


def score_kernel(tokens, vocab_hbm, res, listed, tok_v, side_v, w_v, tok_sem, side_sem, w_sem):
    groups = len(tokens)
    rows = tok_v.shape[0] // groups
    passages = rows // SEQ
    shards, terms = w_v.shape[:2]
    per_device = terms // BLOCK
    tok_dma, side_dma = [], []
    for g, t in enumerate(tokens):
        tok_dma.append(
            pltpu.make_async_copy(
                t.at[pl.ds(0, rows), :], tok_v.at[pl.ds(g * rows, rows), :], tok_sem.at[g]
            )
        )
        side_dma.append(
            pltpu.make_async_copy(
                t.at[pl.ds(rows, EXTRA), pl.ds(0, BLOCK)], side_v.at[g], side_sem.at[g]
            )
        )

    def shard(s):
        at = pl.ds(s * terms if isinstance(s, int) else pl.multiple_of(s * terms, terms), terms)
        return pltpu.make_async_copy(vocab_hbm.at[at, :], w_v.at[s], w_sem.at[s])

    for d in side_dma + tok_dma:
        d.start()
    for s in range(shards):
        shard(s).start()
    y, _, _ = here()
    source = lax.broadcasted_iota(I32, (BLOCK, terms), 0)
    target = lax.div(lax.broadcasted_iota(I32, (BLOCK, terms), 1), BLOCK)
    for d in side_dma:
        d.wait()
    side = jnp.concatenate([side_v[g].astype(F32)[:passages] for g in range(groups)], axis=0)
    side = side.astype(BF16)

    for s in range(shards):
        spread = (source == target + (y * shards + s) * per_device).astype(F32).astype(BF16)
        listed[s] = jnp.dot(side, spread, preferred_element_type=F32)

    for d in tok_dma:
        d.wait()

    @pl.loop(0, shards // GROUP)
    def _(step):
        for k in range(GROUP):
            shard(step * GROUP + k).wait()
        for k in range(GROUP):
            s = step * GROUP + k
            for n in range(terms // STEP):
                at = slice(n * STEP, (n + 1) * STEP)
                logits = lax.dot_general(
                    tok_v[...], w_v[s, at, :], (((1,), (1,)), ((), ())),
                    preferred_element_type=F32,
                )
                best = jnp.max(logits.reshape(groups * passages, SEQ, STEP), axis=1)
                res[s, :, at] = jnp.where(listed[s, :, at] > 0.5, best, FILL)


def score(tokens, vocab, earlier):
    groups = len(tokens)
    rows, width = tokens[0].shape
    rows -= EXTRA
    shards = 2 * NX
    terms = vocab.shape[0] // shards
    part = groups * rows // SEQ
    last = earlier is not None

    def kernel(*refs):
        toks, voc, refs = refs[:groups], refs[groups], refs[groups + 1 :]
        if not last:
            score_kernel(toks, voc, *refs)
            return
        before, outs, res = refs[0], refs[1 : 1 + shards], refs[1 + shards]
        score_kernel(toks, voc, *refs[1 + shards :])
        _, x, core = here()
        for k, (dx, dc) in enumerate(PEERS):
            spot = lax.rem(x + dx, NX) * 2 + lax.rem(core + dc, 2)
            outs[k][:part, :] = before[spot]
            outs[k][part:, :] = res[spot]

    flops = 2 * groups * rows * width * terms * shards
    whole = jax.ShapeDtypeStruct((shards, part, terms), F32)
    piece = jax.ShapeDtypeStruct((PARTS * part, terms), F32)
    return pl.pallas_call(
        kernel,
        out_shape=(piece,) * shards if last else whole,
        in_specs=[hbm()] * (groups + 1) + [vmem()] * last,
        out_specs=(vmem(),) * shards if last else vmem(),
        scratch_shapes=[pltpu.VMEM(whole.shape, F32)] * (1 + last) + [
            pltpu.VMEM((groups * rows, width), BF16),
            pltpu.VMEM((groups, EXTRA, BLOCK), BF16),
            pltpu.VMEM((shards, terms, width), BF16),
            pltpu.SemaphoreType.DMA((groups,)),
            pltpu.SemaphoreType.DMA((groups,)),
            pltpu.SemaphoreType.DMA((shards,)),
        ],
        compiler_params=pltpu.CompilerParams(vmem_limit_bytes=VMEM_BYTES),
        cost_estimate=pl.CostEstimate(
            flops=flops, transcendentals=0, bytes_accessed=shards * terms * width * 2
        ),
        name="score",
    )(*tokens, vocab, *((earlier,) if last else ()))


def finish_kernel(bias_ref, *refs):
    pieces, (out_ref, best) = refs[: len(PEERS)], refs[len(PEERS) :]
    y, x, core = here()
    bias = bias_ref[...].astype(F32).reshape(1, -1)
    share = pieces[0].shape[0] // PARTS
    few = share // NY
    for k in range(0, len(PEERS), 2):
        dx = PEERS[k][0]
        for g, dy in enumerate(OFFSETS):
            same, other = (
                [pieces[k + c][h * share + g * few : h * share + (g + 1) * few, :] for h in range(PARTS)]
                for c in range(2)
            )
            tile = jnp.where(
                core == 0,
                jnp.concatenate(same + other, axis=0),
                jnp.concatenate(other + same, axis=0),
            )
            spot = lax.rem(y + dy, NY) * NX + lax.rem(x + dx, NX)
            best[pl.ds(pl.multiple_of(spot * 8, 8), 8), :] = tile
    out_ref[...] = jnp.log1p(jnp.maximum(best[...] + bias, 0.0)).astype(BF16)


def finish(bias, pieces):
    terms = bias.shape[0]
    rows = NX * NY * 8
    return pl.pallas_call(
        finish_kernel,
        out_shape=jax.ShapeDtypeStruct((rows, terms), BF16),
        in_specs=[vmem()] * (1 + len(pieces)),
        out_specs=vmem(),
        scratch_shapes=[pltpu.VMEM((rows, terms), F32)],
        name="finish",
    )(bias, *pieces)


def shift(value, dy, dx, dc):
    pairs = []
    for y in range(NY):
        for x in range(NX):
            for c in range(2):
                source = (((y + dy) % NY) * NX + (x + dx) % NX) * 2 + (c ^ dc)
                pairs.append((source, (y * NX + x) * 2 + c))
    return lax.ppermute(value, "term", pairs)


def body(
    hidden_states,
    lengths,
    block_list,
    cluster_ids,
    attn_weight,
    out_weight,
    up_weight,
    down_weight,
    head_weight,
    head_gain,
    vocab_weight,
    vocab_bias,
    centroids,
):
    devices = lax.axis_size("grp") * lax.axis_size("term")
    passages = lengths.shape[0]

    side = 2 * NX
    rows_of_chips = [[g * side + k for k in range(side)] for g in range(NY)]
    vocab = lax.all_gather(
        vocab_weight, "term", axis=0, tiled=True, axis_index_groups=rows_of_chips
    )
    first = attend(hidden_states, lengths, attn_weight, out_weight)
    dense, received = [], []
    for part in range(PARTS):
        payload, rows = forward(
            part, first, lengths, block_list, head_gain, up_weight, down_weight, head_weight
        )
        dense.append(rows)
        received.append([payload] + [shift(payload, d, 0, 0) for d in OFFSETS[1:]])

    recv = lax.all_to_all(
        route(cluster_ids, dense, devices), ("grp", "term"), split_axis=0, concat_axis=0, tiled=True
    )


    scored = score(received[0], vocab, None)
    sent = score(received[1], vocab, scored)
    pieces = []
    for dx, dc in PEERS:
        back = sent[PEERS.index(((NX - dx) % NX, dc))]
        pieces.append(back if (dx, dc) == (0, 0) else shift(back, 0, dx, dc))
    sparse = finish(vocab_bias, pieces)
    dense_part, slot_part = place(recv, centroids, passages)
    return (sparse, dense_part[None], slot_part[:, :CAP])


def solution(mesh):
    placed = (
        P(("grp", "term"), None),
        P(("grp", "term")),
        P(("grp", "term"), None),
        P(("grp", "term")),
        P(),
        P(),
        P(),
        P(),
        P(),
        P(),
        P("term", None),
        P("term"),
        P(("grp", "term"), None),
    )
    return jax.shard_map(
        body,
        mesh=mesh,
        in_specs=placed,
        out_specs=(P("grp", "term"), P(("grp", "term"), None, None), P(("grp", "term"), None)),
        check_vma=False,
    )
```

```python
import functools
import math

import jax
import jax.numpy as jnp
from jax import lax
from jax.experimental import pallas as pl
from jax.experimental.pallas import tpu as pltpu
from jax.sharding import PartitionSpec as P

HEAD = 64
BLOCK = 128
SEQ = 128
CL_DEV = 512
CAP = 16
NX = 4
NY = 4
FCH = 512
EXTRA = 16
META = 128
STEP = 256
GROUP = 4
PARTS = 2
OFFSETS = (0, 1, 3, 2)
PEERS = tuple((dx, dc) for dx in OFFSETS for dc in (0, 1))
FILL = -1e30
F32 = jnp.float32
BF16 = jnp.bfloat16
I32 = jnp.int32
VMEM_BYTES = 62 * 1024 * 1024

TAIL = (
    -0.9999988675117493,
    -1.151123285293579,
    -0.4591154456138611,
    -0.05271419882774353,
    0.007333385292440653,
    -0.0003233428578823805,
    -0.00011446241842349991,
    2.508325815142598e-05,
    -1.6903979940252611e-06,
)


def vmem():
    return pl.BlockSpec(memory_space=pltpu.VMEM)


def smem():
    return pl.BlockSpec(memory_space=pltpu.SMEM)


def hbm():
    return pl.BlockSpec(memory_space=pltpu.HBM)


def gelu(x):
    mag = jnp.abs(x)
    power = jnp.full_like(mag, TAIL[-1])
    for coefficient in TAIL[-2::-1]:
        power = power * mag + coefficient
    return jnp.maximum(x, 0.0) - mag * jnp.exp2(power)


def normalize(values):
    width = values.shape[-1]
    center = values - jnp.sum(values, axis=-1, keepdims=True) * (1.0 / width)
    spread = jnp.sum(center * center, axis=-1, keepdims=True) * (1.0 / width)
    return center * lax.rsqrt(spread + 1e-06)


def feed(
    offset, lengths_ref, lists_ref, gain_ref, send_ref, first, up_v, down_v, head_v, wide, acc, waits
):
    rows, width = first.shape
    passages = rows // SEQ
    chunks = up_v.shape[0]
    half = chunks // 2

    def up(c):
        return jnp.dot(first[...], up_v[c], preferred_element_type=F32)

    for part, ready in zip((0, half), waits):
        for d in ready:
            d.wait()
        current = up(part)
        for c in range(part, part + half):
            following = up(c + 1) if c + 1 < part + half else None
            wide[:, c * FCH : (c + 1) * FCH] = gelu(current).astype(BF16)
            current = following
    second = first[...].astype(F32) + jnp.dot(
        wide[...], down_v[...], preferred_element_type=F32
    )
    layer_out = normalize(second).astype(BF16)
    first[...] = layer_out
    middle = gelu(jnp.dot(layer_out, head_v[...], preferred_element_type=F32))
    acc[...] = normalize(middle) * gain_ref[...].reshape(1, width)

    row = lax.broadcasted_iota(I32, (SEQ, 1), 0)
    slots = lists_ref.shape[1]
    block_id = lax.broadcasted_iota(I32, (BLOCK, slots), 0)
    send_ref[rows:, :] = jnp.zeros((EXTRA, width), BF16)
    for p in range(passages):
        base = p * SEQ
        send_ref[base : base + SEQ, :] = jnp.where(
            row < lengths_ref[offset + p], acc[base : base + SEQ, :], acc[base : base + 1, :]
        ).astype(BF16)
        hit = (lists_ref[offset + p : offset + p + 1, :] == block_id).astype(F32).astype(BF16)
        count = lax.dot_general(
            jnp.ones((8, slots), BF16), hit, (((1,), (1,)), ((), ())), preferred_element_type=F32
        )
        send_ref[rows + p : rows + p + 1, 0:BLOCK] = count[0:1, :].astype(BF16)


def feed_moves(up_hbm, down_hbm, head_hbm, up_v, down_v, head_v):
    moves = [
        (up_hbm.at[:, pl.ds(c * FCH, FCH)], up_v.at[c]) for c in range(up_v.shape[0])
    ]
    return moves + [(down_hbm, down_v), (head_hbm, head_v)]


def feed_scratch(rows, width, ff):
    return [
        pltpu.VMEM((rows, width), BF16),
        pltpu.VMEM((ff // FCH, width, FCH), BF16),
        pltpu.VMEM((ff, width), BF16),
        pltpu.VMEM((width, width), BF16),
        pltpu.VMEM((rows, ff), BF16),
        pltpu.VMEM((rows, width), F32),
    ]


def start(moves, sems):
    dma = [pltpu.make_async_copy(s, d, sems.at[i]) for i, (s, d) in enumerate(moves)]
    for d in dma:
        d.start()
    return dma


def lead_kernel(
    lengths_ref, hidden_hbm, lists_ref, gain_ref, attn_hbm, out_hbm, up_hbm, down_hbm, head_hbm,
    send_ref, dense_ref, rest_ref,
    hidden, attn_v, out_v, joined, context, first, up_v, down_v, head_v, wide, acc, sems,
):
    rows, width = hidden.shape
    passages = rows // SEQ
    lead = first.shape[0] // SEQ
    pairs = width // 128
    moves = [(hidden_hbm, hidden)]
    for k in range(3):
        moves.append((attn_hbm.at[:, pl.ds(k * width, width)], attn_v.at[k]))
    moves.append((out_hbm, out_v))
    dma = start(
        moves + feed_moves(up_hbm, down_hbm, head_hbm, up_v, down_v, head_v), sems
    )
    dma[0].wait()
    dma[1].wait()
    for k in range(3):
        if k == 1:
            for d in dma[2:5]:
                d.wait()
        joined[:, k * width : (k + 1) * width] = jnp.dot(
            hidden[...], attn_v[k], preferred_element_type=F32
        ).astype(BF16)

    low = lax.broadcasted_iota(I32, (SEQ, 128), 1) < HEAD
    lane = lax.broadcasted_iota(I32, (2 * SEQ, 128), 1)
    scale = math.log2(math.e) / math.sqrt(HEAD)
    for p in range(passages):
        at = slice(p * SEQ, (p + 1) * SEQ)
        length = lengths_ref[p]
        for h in range(pairs):
            q = joined[at, h * 128 : (h + 1) * 128]
            k = joined[at, width + h * 128 : width + (h + 1) * 128]
            v = joined[at, 2 * width + h * 128 : 2 * width + (h + 1) * 128]
            zero = jnp.zeros_like(q)
            both = jnp.concatenate([jnp.where(low, q, zero), jnp.where(low, zero, q)], axis=0)
            s = lax.dot_general(both, k, (((1,), (1,)), ((), ())), preferred_element_type=F32)
            s = jnp.where(lane < length, s, FILL)
            top = jnp.max(s, axis=-1, keepdims=True)
            e = jnp.exp2((s - top) * scale)
            total = 1.0 / jnp.sum(e, axis=-1, keepdims=True)
            o = jnp.dot(e.astype(BF16), v, preferred_element_type=F32)
            mix = jnp.where(low, o[:SEQ] * total[:SEQ], o[SEQ:] * total[SEQ:])
            context[at, h * 128 : (h + 1) * 128] = mix.astype(BF16)

    for p in range(passages):
        at = slice(p * SEQ, (p + 1) * SEQ)
        mixed = hidden[at, :].astype(F32) + jnp.dot(
            context[at, :], out_v[...], preferred_element_type=F32
        )
        into, k = (first, p) if p < lead else (rest_ref, p - lead)
        into[k * SEQ : (k + 1) * SEQ, :] = normalize(mixed).astype(BF16)

    feed(
        0, lengths_ref, lists_ref, gain_ref, send_ref, first, up_v, down_v, head_v, wide, acc,
        (dma[5:], ()),
    )
    for p in range(lead):
        dense_ref[p : p + 1, :] = first[p * SEQ : p * SEQ + 1, :].astype(F32)


def encode_lead(hidden, lengths, block_list, gain, attn_w, out_w, up_w, down_w, head_w):
    rows, width = hidden.shape
    part = rows // PARTS
    ff = up_w.shape[1]
    return pl.pallas_call(
        lead_kernel,
        out_shape=(
            jax.ShapeDtypeStruct((part + EXTRA, width), BF16),
            jax.ShapeDtypeStruct((8, width), F32),
            jax.ShapeDtypeStruct((rows - part, width), BF16),
        ),
        in_specs=[smem(), hbm(), vmem(), vmem()] + [hbm()] * 5,
        out_specs=(vmem(), vmem(), vmem()),
        scratch_shapes=[
            pltpu.VMEM((rows, width), BF16),
            pltpu.VMEM((3, width, width), BF16),
            pltpu.VMEM((width, width), BF16),
            pltpu.VMEM((rows, 3 * width), BF16),
            pltpu.VMEM((rows, width), BF16),
        ] + feed_scratch(part, width, ff) + [pltpu.SemaphoreType.DMA((7 + ff // FCH,))],
        compiler_params=pltpu.CompilerParams(vmem_limit_bytes=VMEM_BYTES),
        cost_estimate=pl.CostEstimate(
            flops=2 * rows * width * 4 * width, transcendentals=0, bytes_accessed=8 * width * width
        ),
        name="lead",
    )(lengths, hidden, block_list, gain, attn_w, out_w, up_w, down_w, head_w)


def tail_kernel(
    lengths_ref, clusters_ref, rest_hbm, lists_ref, gain_ref, dense_ref, up_hbm, down_hbm, head_hbm,
    send_ref, route_ref,
    first, up_v, down_v, head_v, wide, acc, sems,
):
    rows, width = first.shape
    lead = clusters_ref.shape[0] - rows // SEQ
    half = up_v.shape[0] // 2
    dma = start(
        [(rest_hbm, first)] + feed_moves(up_hbm, down_hbm, head_hbm, up_v, down_v, head_v), sems
    )
    feed(
        lead, lengths_ref, lists_ref, gain_ref, send_ref, first, up_v, down_v, head_v, wide, acc,
        (dma[: 1 + half], dma[1 + half :]),
    )
    dense = [dense_ref[p : p + 1, :] for p in range(lead)]
    dense += [first[p : p + 1, :].astype(F32) for p in range(0, rows, SEQ)]

    devices = route_ref.shape[0]
    pieces = width // META
    row = lax.broadcasted_iota(I32, (devices, 1), 0)
    lane = lax.broadcasted_iota(I32, (devices, META), 1)
    term = lax.axis_index("term").astype(I32)
    device = lax.axis_index("grp").astype(I32) * lax.axis_size("term") + term
    parts = [jnp.zeros((devices, META), F32) for _ in range(pieces)]
    meta = jnp.zeros((devices, META), I32)
    for p, values in enumerate(dense):
        cluster = clusters_ref[p]
        owner = lax.div(cluster, CL_DEV)
        mine = row == owner
        for k in range(pieces):
            parts[k] = jnp.where(mine, values[:, k * META : (k + 1) * META], parts[k])
        word = jnp.where(lane == 0, 1, 0)
        word = jnp.where(lane == 1, device, word)
        word = jnp.where(lane == 2, p, word)
        word = jnp.where(lane == 3, cluster - owner * CL_DEV, word)
        meta = jnp.where(mine, word, meta)
    for k in range(pieces):
        route_ref[:, k, :] = parts[k]
    route_ref[:, pieces, :] = meta.astype(F32)
    route_ref[:, pieces + 1, :] = jnp.zeros((devices, META), F32)


def encode_tail(rest, lengths, clusters, block_list, gain, dense, up_w, down_w, head_w, devices):
    rows, width = rest.shape
    ff = up_w.shape[1]
    return pl.pallas_call(
        tail_kernel,
        out_shape=(
            jax.ShapeDtypeStruct((rows + EXTRA, width), BF16),
            jax.ShapeDtypeStruct((devices, 8, META), F32),
        ),
        in_specs=[smem(), smem(), hbm(), vmem(), vmem(), vmem(), hbm(), hbm(), hbm()],
        out_specs=(vmem(), vmem()),
        scratch_shapes=feed_scratch(rows, width, ff)
        + [pltpu.SemaphoreType.DMA((3 + ff // FCH,))],
        compiler_params=pltpu.CompilerParams(vmem_limit_bytes=VMEM_BYTES),
        cost_estimate=pl.CostEstimate(flops=1, transcendentals=0, bytes_accessed=1),
        name="tail",
    )(lengths, clusters, rest, block_list, gain, dense, up_w, down_w, head_w)


def here():
    term = lax.axis_index("term").astype(I32)
    chip = lax.div(term, 2)
    return lax.div(chip, NX), lax.rem(chip, NX), lax.rem(term, 2)


def place_kernel(passages, recv_ref, cent_ref, dense_ref, slot_ref):
    devices = recv_ref.shape[0]
    width = dense_ref.shape[1]
    pieces = width // META
    words = recv_ref[:, pieces, :]
    high = jnp.floor(words * (1.0 / 256.0))
    meta = words.astype(BF16)
    source = lax.broadcasted_iota(I32, (devices, devices), 0)
    other = lax.broadcasted_iota(I32, (devices, devices), 1)
    before = (other < source).astype(F32).astype(BF16)
    valid = words[:, 0:1]
    rank = jnp.dot(before, meta, preferred_element_type=F32)[:, 0:1]
    slot = lax.broadcasted_iota(I32, (devices, META), 1).astype(F32)
    chosen = ((rank == slot) & (valid > 0.5)).astype(F32).astype(BF16)
    over = (((0,), (0,)), ((), ()))

    def pick(values):
        return lax.dot_general(
            chosen, values.astype(BF16), over, preferred_element_type=F32
        )[:CAP]

    small = pick(words - high * 256.0)
    large = pick(high)
    filled = small[:, 0:1] > 0.5
    local = (small + large * 256.0)[:, 3:4]
    ids = lax.broadcasted_iota(I32, (CAP, cent_ref.shape[0]), 1).astype(F32)
    lookup = ((ids == local) & filled).astype(F32).astype(BF16)
    center = jnp.dot(lookup, cent_ref[...], preferred_element_type=F32)
    for k in range(pieces):
        at = slice(k * META, (k + 1) * META)
        dense_ref[:, at] = jnp.where(
            filled, pick(recv_ref[:, k, :]) - center[:, at], 0.0
        ).astype(BF16)
    names = lax.dot_general(meta, chosen, over, preferred_element_type=F32)
    ident = names[1:2, :] * passages + names[2:3, :]
    slot_ref[...] = jnp.where(names[0:1, :] > 0.5, ident, -1.0).astype(I32)


def place(recv, centroids, passages):
    width = centroids.shape[1]
    return pl.pallas_call(
        functools.partial(place_kernel, passages),
        out_shape=(
            jax.ShapeDtypeStruct((CAP, width), BF16),
            jax.ShapeDtypeStruct((1, META), I32),
        ),
        in_specs=[vmem(), vmem()],
        out_specs=(vmem(), vmem()),
        name="place",
    )(recv, centroids)


def score_kernel(tokens, vocab_hbm, res, listed, tok_v, side_v, w_v, tok_sem, side_sem, w_sem):
    groups = len(tokens)
    rows = tok_v.shape[0] // groups
    passages = rows // SEQ
    shards, terms = w_v.shape[:2]
    per_device = terms // BLOCK
    tok_dma, side_dma = [], []
    for g, t in enumerate(tokens):
        tok_dma.append(
            pltpu.make_async_copy(
                t.at[pl.ds(0, rows), :], tok_v.at[pl.ds(g * rows, rows), :], tok_sem.at[g]
            )
        )
        side_dma.append(
            pltpu.make_async_copy(
                t.at[pl.ds(rows, EXTRA), pl.ds(0, BLOCK)], side_v.at[g], side_sem.at[g]
            )
        )

    def shard(s):
        at = pl.ds(s * terms if isinstance(s, int) else pl.multiple_of(s * terms, terms), terms)
        return pltpu.make_async_copy(vocab_hbm.at[at, :], w_v.at[s], w_sem.at[s])

    for d in side_dma + tok_dma:
        d.start()
    for s in range(shards):
        shard(s).start()
    y, _, _ = here()
    source = lax.broadcasted_iota(I32, (BLOCK, terms), 0)
    target = lax.div(lax.broadcasted_iota(I32, (BLOCK, terms), 1), BLOCK)
    for d in side_dma:
        d.wait()
    side = jnp.concatenate([side_v[g].astype(F32)[:passages] for g in range(groups)], axis=0)
    side = side.astype(BF16)

    for s in range(shards):
        spread = (source == target + (y * shards + s) * per_device).astype(F32).astype(BF16)
        listed[s] = jnp.dot(side, spread, preferred_element_type=F32)

    for d in tok_dma:
        d.wait()

    @pl.loop(0, shards // GROUP)
    def _(step):
        for k in range(GROUP):
            shard(step * GROUP + k).wait()
        for k in range(GROUP):
            s = step * GROUP + k
            for n in range(terms // STEP):
                at = slice(n * STEP, (n + 1) * STEP)
                logits = lax.dot_general(
                    tok_v[...], w_v[s, at, :], (((1,), (1,)), ((), ())),
                    preferred_element_type=F32,
                )
                best = jnp.max(logits.reshape(groups * passages, SEQ, STEP), axis=1)
                res[s, :, at] = jnp.where(listed[s, :, at] > 0.5, best, FILL)


def score(tokens, vocab, earlier):
    groups = len(tokens)
    rows, width = tokens[0].shape
    rows -= EXTRA
    shards = 2 * NX
    terms = vocab.shape[0] // shards
    part = groups * rows // SEQ
    last = earlier is not None

    def kernel(*refs):
        toks, voc, refs = refs[:groups], refs[groups], refs[groups + 1 :]
        if not last:
            score_kernel(toks, voc, *refs)
            return
        before, outs, res = refs[0], refs[1 : 1 + shards], refs[1 + shards]
        score_kernel(toks, voc, *refs[1 + shards :])
        _, x, core = here()
        for k, (dx, dc) in enumerate(PEERS):
            spot = lax.rem(x + dx, NX) * 2 + lax.rem(core + dc, 2)
            outs[k][:part, :] = before[spot]
            outs[k][part:, :] = res[spot]

    flops = 2 * groups * rows * width * terms * shards
    whole = jax.ShapeDtypeStruct((shards, part, terms), F32)
    piece = jax.ShapeDtypeStruct((PARTS * part, terms), F32)
    return pl.pallas_call(
        kernel,
        out_shape=(piece,) * shards if last else whole,
        in_specs=[hbm()] * (groups + 1) + [vmem()] * last,
        out_specs=(vmem(),) * shards if last else vmem(),
        scratch_shapes=[pltpu.VMEM(whole.shape, F32)] * (1 + last) + [
            pltpu.VMEM((groups * rows, width), BF16),
            pltpu.VMEM((groups, EXTRA, BLOCK), BF16),
            pltpu.VMEM((shards, terms, width), BF16),
            pltpu.SemaphoreType.DMA((groups,)),
            pltpu.SemaphoreType.DMA((groups,)),
            pltpu.SemaphoreType.DMA((shards,)),
        ],
        compiler_params=pltpu.CompilerParams(vmem_limit_bytes=VMEM_BYTES),
        cost_estimate=pl.CostEstimate(
            flops=flops, transcendentals=0, bytes_accessed=shards * terms * width * 2
        ),
        name="score",
    )(*tokens, vocab, *((earlier,) if last else ()))


def finish_kernel(bias_ref, *refs):
    pieces, (out_ref, best) = refs[: len(PEERS)], refs[len(PEERS) :]
    y, x, core = here()
    bias = bias_ref[...].astype(F32).reshape(1, -1)
    share = pieces[0].shape[0] // PARTS
    few = share // NY
    for k in range(0, len(PEERS), 2):
        dx = PEERS[k][0]
        for g, dy in enumerate(OFFSETS):
            same, other = (
                [pieces[k + c][h * share + g * few : h * share + (g + 1) * few, :] for h in range(PARTS)]
                for c in range(2)
            )
            tile = jnp.where(
                core == 0,
                jnp.concatenate(same + other, axis=0),
                jnp.concatenate(other + same, axis=0),
            )
            spot = lax.rem(y + dy, NY) * NX + lax.rem(x + dx, NX)
            best[pl.ds(pl.multiple_of(spot * 8, 8), 8), :] = tile
    out_ref[...] = jnp.log1p(jnp.maximum(best[...] + bias, 0.0)).astype(BF16)


def finish(bias, pieces):
    terms = bias.shape[0]
    rows = NX * NY * 8
    return pl.pallas_call(
        finish_kernel,
        out_shape=jax.ShapeDtypeStruct((rows, terms), BF16),
        in_specs=[vmem()] * (1 + len(pieces)),
        out_specs=vmem(),
        scratch_shapes=[pltpu.VMEM((rows, terms), F32)],
        name="finish",
    )(bias, *pieces)


def shift(value, dy, dx, dc):
    pairs = []
    for y in range(NY):
        for x in range(NX):
            for c in range(2):
                source = (((y + dy) % NY) * NX + (x + dx) % NX) * 2 + (c ^ dc)
                pairs.append((source, (y * NX + x) * 2 + c))
    return lax.ppermute(value, "term", pairs)


def body(
    hidden_states,
    lengths,
    block_list,
    cluster_ids,
    attn_weight,
    out_weight,
    up_weight,
    down_weight,
    head_weight,
    head_gain,
    vocab_weight,
    vocab_bias,
    centroids,
):
    devices = lax.axis_size("grp") * lax.axis_size("term")
    passages = lengths.shape[0]

    side = 2 * NX
    rows_of_chips = [[g * side + k for k in range(side)] for g in range(NY)]
    vocab = lax.all_gather(
        vocab_weight, "term", axis=0, tiled=True, axis_index_groups=rows_of_chips
    )
    def spread(payload):
        return [payload] + [shift(payload, d, 0, 0) for d in OFFSETS[1:]]

    payload, dense, rest = encode_lead(
        hidden_states, lengths, block_list, head_gain,
        attn_weight, out_weight, up_weight, down_weight, head_weight,
    )
    early = spread(payload)
    payload, routed = encode_tail(
        rest, lengths, cluster_ids, block_list, head_gain, dense,
        up_weight, down_weight, head_weight, devices,
    )
    late = spread(payload)
    recv = lax.all_to_all(routed, ("grp", "term"), split_axis=0, concat_axis=0, tiled=True)

    scored = score(early, vocab, None)
    dense_part, slot_part = place(recv, centroids, passages)
    scored, dense_part, slot_part = lax.optimization_barrier((scored, dense_part, slot_part))
    sent = score(late, vocab, scored)
    pieces = []
    for dx, dc in PEERS:
        back = sent[PEERS.index(((NX - dx) % NX, dc))]
        pieces.append(back if (dx, dc) == (0, 0) else shift(back, 0, dx, dc))
    sparse = finish(vocab_bias, pieces)
    return (sparse, dense_part[None], slot_part[:, :CAP])


def solution(mesh):
    placed = (
        P(("grp", "term"), None),
        P(("grp", "term")),
        P(("grp", "term"), None),
        P(("grp", "term")),
        P(),
        P(),
        P(),
        P(),
        P(),
        P(),
        P("term", None),
        P("term"),
        P(("grp", "term"), None),
    )
    return jax.shard_map(
        body,
        mesh=mesh,
        in_specs=placed,
        out_specs=(P("grp", "term"), P(("grp", "term"), None, None), P(("grp", "term"), None)),
        check_vma=False,
    )
```

```python
import functools
import math

import jax
import jax.numpy as jnp
from jax import lax
from jax.experimental import pallas as pl
from jax.experimental.pallas import tpu as pltpu
from jax.sharding import PartitionSpec as P

HEAD = 64
BLOCK = 128
SEQ = 128
CL_DEV = 512
CAP = 16
NX = 4
NY = 4
FCH = 512
EXTRA = 16
META = 128
STEP = 256
GROUP = 4
PARTS = 2
OFFSETS = (0, 1, 3, 2)
PEERS = tuple((dx, dc) for dx in OFFSETS for dc in (0, 1))
FILL = -1e30
F32 = jnp.float32
BF16 = jnp.bfloat16
I32 = jnp.int32
VMEM_BYTES = 62 * 1024 * 1024

TAIL = (
    -0.9999988675117493,
    -1.151123285293579,
    -0.4591154456138611,
    -0.05271419882774353,
    0.007333385292440653,
    -0.0003233428578823805,
    -0.00011446241842349991,
    2.508325815142598e-05,
    -1.6903979940252611e-06,
)


def vmem():
    return pl.BlockSpec(memory_space=pltpu.VMEM)


def smem():
    return pl.BlockSpec(memory_space=pltpu.SMEM)


def hbm():
    return pl.BlockSpec(memory_space=pltpu.HBM)


def gelu(x):
    mag = jnp.abs(x)
    power = jnp.full_like(mag, TAIL[-1])
    for coefficient in TAIL[-2::-1]:
        power = power * mag + coefficient
    return jnp.maximum(x, 0.0) - mag * jnp.exp2(power)


def normalize(values):
    width = values.shape[-1]
    center = values - jnp.sum(values, axis=-1, keepdims=True) * (1.0 / width)
    spread = jnp.sum(center * center, axis=-1, keepdims=True) * (1.0 / width)
    return center * lax.rsqrt(spread + 1e-06)


def feed(
    offset, lengths_ref, lists_ref, gain_ref, send_ref, first, up_v, down_v, head_v, wide, acc, waits
):
    rows, width = first.shape
    passages = rows // SEQ
    chunks = up_v.shape[0]
    half = chunks // 2

    def up(c):
        return jnp.dot(first[...], up_v[c], preferred_element_type=F32)

    for part, ready in zip((0, half), waits):
        for d in ready:
            d.wait()
        current = up(part)
        for c in range(part, part + half):
            following = up(c + 1) if c + 1 < part + half else None
            wide[:, c * FCH : (c + 1) * FCH] = gelu(current).astype(BF16)
            current = following
    second = first[...].astype(F32) + jnp.dot(
        wide[...], down_v[...], preferred_element_type=F32
    )
    layer_out = normalize(second).astype(BF16)
    first[...] = layer_out
    middle = gelu(jnp.dot(layer_out, head_v[...], preferred_element_type=F32))
    acc[...] = normalize(middle) * gain_ref[...].reshape(1, width)

    row = lax.broadcasted_iota(I32, (SEQ, 1), 0)
    slots = lists_ref.shape[1]
    block_id = lax.broadcasted_iota(I32, (BLOCK, slots), 0)
    send_ref[rows:, :] = jnp.zeros((EXTRA, width), BF16)
    for p in range(passages):
        base = p * SEQ
        send_ref[base : base + SEQ, :] = jnp.where(
            row < lengths_ref[offset + p], acc[base : base + SEQ, :], acc[base : base + 1, :]
        ).astype(BF16)
        hit = (lists_ref[offset + p : offset + p + 1, :] == block_id).astype(F32).astype(BF16)
        count = lax.dot_general(
            jnp.ones((8, slots), BF16), hit, (((1,), (1,)), ((), ())), preferred_element_type=F32
        )
        send_ref[rows + p : rows + p + 1, 0:BLOCK] = count[0:1, :].astype(BF16)


def feed_moves(up_hbm, down_hbm, head_hbm, up_v, down_v, head_v):
    moves = [
        (up_hbm.at[:, pl.ds(c * FCH, FCH)], up_v.at[c]) for c in range(up_v.shape[0])
    ]
    return moves + [(down_hbm, down_v), (head_hbm, head_v)]


def feed_scratch(rows, width, ff):
    return [
        pltpu.VMEM((rows, width), BF16),
        pltpu.VMEM((ff // FCH, width, FCH), BF16),
        pltpu.VMEM((ff, width), BF16),
        pltpu.VMEM((width, width), BF16),
        pltpu.VMEM((rows, ff), BF16),
        pltpu.VMEM((rows, width), F32),
    ]


def start(moves, sems):
    dma = [pltpu.make_async_copy(s, d, sems.at[i]) for i, (s, d) in enumerate(moves)]
    for d in dma:
        d.start()
    return dma


def lead_kernel(
    lengths_ref, hidden_hbm, lists_ref, gain_ref, attn_hbm, out_hbm, up_hbm, down_hbm, head_hbm,
    send_ref, dense_ref, rest_ref,
    hidden, attn_v, out_v, joined, context, first, up_v, down_v, head_v, wide, acc, sems,
):
    rows, width = hidden.shape
    passages = rows // SEQ
    lead = first.shape[0] // SEQ
    pairs = width // 128
    moves = [(hidden_hbm, hidden)]
    for k in range(3):
        moves.append((attn_hbm.at[:, pl.ds(k * width, width)], attn_v.at[k]))
    moves.append((out_hbm, out_v))
    dma = start(
        moves + feed_moves(up_hbm, down_hbm, head_hbm, up_v, down_v, head_v), sems
    )
    dma[0].wait()
    dma[1].wait()
    for k in range(3):
        if k == 1:
            for d in dma[2:5]:
                d.wait()
        joined[:, k * width : (k + 1) * width] = jnp.dot(
            hidden[...], attn_v[k], preferred_element_type=F32
        ).astype(BF16)

    low = lax.broadcasted_iota(I32, (SEQ, 128), 1) < HEAD
    lane = lax.broadcasted_iota(I32, (2 * SEQ, 128), 1)
    scale = math.log2(math.e) / math.sqrt(HEAD)
    for p in range(passages):
        at = slice(p * SEQ, (p + 1) * SEQ)
        length = lengths_ref[p]
        for h in range(pairs):
            q = joined[at, h * 128 : (h + 1) * 128]
            k = joined[at, width + h * 128 : width + (h + 1) * 128]
            v = joined[at, 2 * width + h * 128 : 2 * width + (h + 1) * 128]
            zero = jnp.zeros_like(q)
            both = jnp.concatenate([jnp.where(low, q, zero), jnp.where(low, zero, q)], axis=0)
            s = lax.dot_general(both, k, (((1,), (1,)), ((), ())), preferred_element_type=F32)
            s = jnp.where(lane < length, s, FILL)
            top = jnp.max(s, axis=-1, keepdims=True)
            e = jnp.exp2((s - top) * scale)
            total = 1.0 / jnp.sum(e, axis=-1, keepdims=True)
            o = jnp.dot(e.astype(BF16), v, preferred_element_type=F32)
            mix = jnp.where(low, o[:SEQ] * total[:SEQ], o[SEQ:] * total[SEQ:])
            context[at, h * 128 : (h + 1) * 128] = mix.astype(BF16)

    for p in range(passages):
        at = slice(p * SEQ, (p + 1) * SEQ)
        mixed = hidden[at, :].astype(F32) + jnp.dot(
            context[at, :], out_v[...], preferred_element_type=F32
        )
        into, k = (first, p) if p < lead else (rest_ref, p - lead)
        into[k * SEQ : (k + 1) * SEQ, :] = normalize(mixed).astype(BF16)

    feed(
        0, lengths_ref, lists_ref, gain_ref, send_ref, first, up_v, down_v, head_v, wide, acc,
        (dma[5:], ()),
    )
    for p in range(lead):
        dense_ref[p : p + 1, :] = first[p * SEQ : p * SEQ + 1, :].astype(F32)


def encode_lead(hidden, lengths, block_list, gain, attn_w, out_w, up_w, down_w, head_w):
    rows, width = hidden.shape
    part = rows // PARTS
    ff = up_w.shape[1]
    return pl.pallas_call(
        lead_kernel,
        out_shape=(
            jax.ShapeDtypeStruct((part + EXTRA, width), BF16),
            jax.ShapeDtypeStruct((8, width), F32),
            jax.ShapeDtypeStruct((rows - part, width), BF16),
        ),
        in_specs=[smem(), hbm(), vmem(), vmem()] + [hbm()] * 5,
        out_specs=(vmem(), vmem(), vmem()),
        scratch_shapes=[
            pltpu.VMEM((rows, width), BF16),
            pltpu.VMEM((3, width, width), BF16),
            pltpu.VMEM((width, width), BF16),
            pltpu.VMEM((rows, 3 * width), BF16),
            pltpu.VMEM((rows, width), BF16),
        ] + feed_scratch(part, width, ff) + [pltpu.SemaphoreType.DMA((7 + ff // FCH,))],
        compiler_params=pltpu.CompilerParams(vmem_limit_bytes=VMEM_BYTES),
        cost_estimate=pl.CostEstimate(
            flops=2 * rows * width * 4 * width, transcendentals=0, bytes_accessed=8 * width * width
        ),
        name="lead",
    )(lengths, hidden, block_list, gain, attn_w, out_w, up_w, down_w, head_w)


def tail_kernel(
    lengths_ref, clusters_ref, rest_hbm, lists_ref, gain_ref, dense_ref, up_hbm, down_hbm, head_hbm,
    send_ref, route_ref,
    first, up_v, down_v, head_v, wide, acc, sems,
):
    rows, width = first.shape
    lead = clusters_ref.shape[0] - rows // SEQ
    half = up_v.shape[0] // 2
    dma = start(
        [(rest_hbm, first)] + feed_moves(up_hbm, down_hbm, head_hbm, up_v, down_v, head_v), sems
    )
    feed(
        lead, lengths_ref, lists_ref, gain_ref, send_ref, first, up_v, down_v, head_v, wide, acc,
        (dma[: 1 + half], dma[1 + half :]),
    )
    dense = [dense_ref[p : p + 1, :] for p in range(lead)]
    dense += [first[p : p + 1, :].astype(F32) for p in range(0, rows, SEQ)]

    devices = route_ref.shape[0]
    pieces = width // META
    row = lax.broadcasted_iota(I32, (devices, 1), 0)
    lane = lax.broadcasted_iota(I32, (devices, META), 1)
    term = lax.axis_index("term").astype(I32)
    device = lax.axis_index("grp").astype(I32) * lax.axis_size("term") + term
    parts = [jnp.zeros((devices, META), F32) for _ in range(pieces)]
    meta = jnp.zeros((devices, META), I32)
    for p, values in enumerate(dense):
        cluster = clusters_ref[p]
        owner = lax.div(cluster, CL_DEV)
        mine = row == owner
        for k in range(pieces):
            parts[k] = jnp.where(mine, values[:, k * META : (k + 1) * META], parts[k])
        word = jnp.where(lane == 0, 1, 0)
        word = jnp.where(lane == 1, device, word)
        word = jnp.where(lane == 2, p, word)
        word = jnp.where(lane == 3, cluster - owner * CL_DEV, word)
        meta = jnp.where(mine, word, meta)
    for k in range(pieces):
        route_ref[:, k, :] = parts[k]
    route_ref[:, pieces, :] = meta.astype(F32)
    route_ref[:, pieces + 1, :] = jnp.zeros((devices, META), F32)


def encode_tail(rest, lengths, clusters, block_list, gain, dense, up_w, down_w, head_w, devices):
    rows, width = rest.shape
    ff = up_w.shape[1]
    return pl.pallas_call(
        tail_kernel,
        out_shape=(
            jax.ShapeDtypeStruct((rows + EXTRA, width), BF16),
            jax.ShapeDtypeStruct((devices, 8, META), F32),
        ),
        in_specs=[smem(), smem(), hbm(), vmem(), vmem(), vmem(), hbm(), hbm(), hbm()],
        out_specs=(vmem(), vmem()),
        scratch_shapes=feed_scratch(rows, width, ff)
        + [pltpu.SemaphoreType.DMA((3 + ff // FCH,))],
        compiler_params=pltpu.CompilerParams(vmem_limit_bytes=VMEM_BYTES),
        cost_estimate=pl.CostEstimate(flops=1, transcendentals=0, bytes_accessed=1),
        name="tail",
    )(lengths, clusters, rest, block_list, gain, dense, up_w, down_w, head_w)


def here():
    term = lax.axis_index("term").astype(I32)
    chip = lax.div(term, 2)
    return lax.div(chip, NX), lax.rem(chip, NX), lax.rem(term, 2)


def place_kernel(passages, recv_ref, cent_ref, dense_ref, slot_ref):
    devices = recv_ref.shape[0]
    width = dense_ref.shape[1]
    pieces = width // META
    words = recv_ref[:, pieces, :]
    high = jnp.floor(words * (1.0 / 256.0))
    meta = words.astype(BF16)
    source = lax.broadcasted_iota(I32, (devices, devices), 0)
    other = lax.broadcasted_iota(I32, (devices, devices), 1)
    before = (other < source).astype(F32).astype(BF16)
    valid = words[:, 0:1]
    rank = jnp.dot(before, meta, preferred_element_type=F32)[:, 0:1]
    slot = lax.broadcasted_iota(I32, (devices, META), 1).astype(F32)
    chosen = ((rank == slot) & (valid > 0.5)).astype(F32).astype(BF16)
    over = (((0,), (0,)), ((), ()))

    def pick(values):
        return lax.dot_general(
            chosen, values.astype(BF16), over, preferred_element_type=F32
        )[:CAP]

    small = pick(words - high * 256.0)
    large = pick(high)
    filled = small[:, 0:1] > 0.5
    local = (small + large * 256.0)[:, 3:4]
    ids = lax.broadcasted_iota(I32, (CAP, cent_ref.shape[0]), 1).astype(F32)
    lookup = ((ids == local) & filled).astype(F32).astype(BF16)
    center = jnp.dot(lookup, cent_ref[...], preferred_element_type=F32)
    for k in range(pieces):
        at = slice(k * META, (k + 1) * META)
        dense_ref[:, at] = jnp.where(
            filled, pick(recv_ref[:, k, :]) - center[:, at], 0.0
        ).astype(BF16)
    names = lax.dot_general(meta, chosen, over, preferred_element_type=F32)
    ident = names[1:2, :] * passages + names[2:3, :]
    slot_ref[...] = jnp.where(names[0:1, :] > 0.5, ident, -1.0).astype(I32)


def place(recv, centroids, passages):
    width = centroids.shape[1]
    return pl.pallas_call(
        functools.partial(place_kernel, passages),
        out_shape=(
            jax.ShapeDtypeStruct((CAP, width), BF16),
            jax.ShapeDtypeStruct((1, META), I32),
        ),
        in_specs=[vmem(), vmem()],
        out_specs=(vmem(), vmem()),
        name="place",
    )(recv, centroids)


def score_kernel(tokens, vocab_hbm, res, listed, tok_v, side_v, w_v, tok_sem, side_sem, w_sem):
    groups = len(tokens)
    rows = tok_v.shape[0] // groups
    passages = rows // SEQ
    shards, terms = w_v.shape[:2]
    per_device = terms // BLOCK
    tok_dma, side_dma = [], []
    for g, t in enumerate(tokens):
        tok_dma.append(
            pltpu.make_async_copy(
                t.at[pl.ds(0, rows), :], tok_v.at[pl.ds(g * rows, rows), :], tok_sem.at[g]
            )
        )
        side_dma.append(
            pltpu.make_async_copy(
                t.at[pl.ds(rows, EXTRA), pl.ds(0, BLOCK)], side_v.at[g], side_sem.at[g]
            )
        )

    def shard(s):
        at = pl.ds(s * terms if isinstance(s, int) else pl.multiple_of(s * terms, terms), terms)
        return pltpu.make_async_copy(vocab_hbm.at[at, :], w_v.at[s], w_sem.at[s])

    for d in side_dma + tok_dma:
        d.start()
    for s in range(shards):
        shard(s).start()
    y, _, _ = here()
    source = lax.broadcasted_iota(I32, (BLOCK, terms), 0)
    target = lax.div(lax.broadcasted_iota(I32, (BLOCK, terms), 1), BLOCK)
    for d in side_dma:
        d.wait()
    side = jnp.concatenate([side_v[g].astype(F32)[:passages] for g in range(groups)], axis=0)
    side = side.astype(BF16)

    for s in range(shards):
        spread = (source == target + (y * shards + s) * per_device).astype(F32).astype(BF16)
        listed[s] = jnp.dot(side, spread, preferred_element_type=F32)

    for d in tok_dma:
        d.wait()

    @pl.loop(0, shards // GROUP)
    def _(step):
        for k in range(GROUP):
            shard(step * GROUP + k).wait()
        for k in range(GROUP):
            s = step * GROUP + k
            for n in range(terms // STEP):
                at = slice(n * STEP, (n + 1) * STEP)
                logits = lax.dot_general(
                    tok_v[...], w_v[s, at, :], (((1,), (1,)), ((), ())),
                    preferred_element_type=F32,
                )
                best = jnp.max(logits.reshape(groups * passages, SEQ, STEP), axis=1)
                res[s, :, at] = jnp.where(listed[s, :, at] > 0.5, best, FILL)


def score(tokens, vocab, earlier):
    groups = len(tokens)
    rows, width = tokens[0].shape
    rows -= EXTRA
    shards = 2 * NX
    terms = vocab.shape[0] // shards
    part = groups * rows // SEQ
    last = earlier is not None

    def kernel(*refs):
        toks, voc, refs = refs[:groups], refs[groups], refs[groups + 1 :]
        if not last:
            score_kernel(toks, voc, *refs)
            return
        before, outs, res = refs[0], refs[1 : 1 + shards], refs[1 + shards]
        score_kernel(toks, voc, *refs[1 + shards :])
        _, x, core = here()
        for k, (dx, dc) in enumerate(PEERS):
            spot = lax.rem(x + dx, NX) * 2 + lax.rem(core + dc, 2)
            outs[k][:done, :] = before[spot]
            outs[k][done:, :] = res[spot]

    flops = 2 * groups * rows * width * terms * shards
    whole = jax.ShapeDtypeStruct((shards, part, terms), F32)
    done = earlier.shape[1] if last else 0
    piece = jax.ShapeDtypeStruct((done + part, terms), F32)
    return pl.pallas_call(
        kernel,
        out_shape=(piece,) * shards if last else whole,
        in_specs=[hbm()] * (groups + 1) + [vmem()] * last,
        out_specs=(vmem(),) * shards if last else vmem(),
        scratch_shapes=[pltpu.VMEM(whole.shape, F32)] * (1 + last) + [
            pltpu.VMEM((groups * rows, width), BF16),
            pltpu.VMEM((groups, EXTRA, BLOCK), BF16),
            pltpu.VMEM((shards, terms, width), BF16),
            pltpu.SemaphoreType.DMA((groups,)),
            pltpu.SemaphoreType.DMA((groups,)),
            pltpu.SemaphoreType.DMA((shards,)),
        ],
        compiler_params=pltpu.CompilerParams(vmem_limit_bytes=VMEM_BYTES),
        cost_estimate=pl.CostEstimate(
            flops=flops, transcendentals=0, bytes_accessed=shards * terms * width * 2
        ),
        name="score",
    )(*tokens, vocab, *((earlier,) if last else ()))


def finish_kernel(bias_ref, *refs):
    pieces, (out_ref, best) = refs[: len(PEERS)], refs[len(PEERS) :]
    y, x, core = here()
    bias = bias_ref[...].astype(F32).reshape(1, -1)
    share = pieces[0].shape[0] // PARTS
    few = share // NY
    for k in range(0, len(PEERS), 2):
        dx = PEERS[k][0]
        for g, dy in enumerate(OFFSETS):
            same, other = (
                [pieces[k + c][h * share + g * few : h * share + (g + 1) * few, :] for h in range(PARTS)]
                for c in range(2)
            )
            tile = jnp.where(
                core == 0,
                jnp.concatenate(same + other, axis=0),
                jnp.concatenate(other + same, axis=0),
            )
            spot = lax.rem(y + dy, NY) * NX + lax.rem(x + dx, NX)
            best[pl.ds(pl.multiple_of(spot * 8, 8), 8), :] = tile
    out_ref[...] = jnp.log1p(jnp.maximum(best[...] + bias, 0.0)).astype(BF16)


def finish(bias, pieces):
    terms = bias.shape[0]
    rows = NX * NY * 8
    return pl.pallas_call(
        finish_kernel,
        out_shape=jax.ShapeDtypeStruct((rows, terms), BF16),
        in_specs=[vmem()] * (1 + len(pieces)),
        out_specs=vmem(),
        scratch_shapes=[pltpu.VMEM((rows, terms), F32)],
        name="finish",
    )(bias, *pieces)


def shift(value, dy, dx, dc):
    pairs = []
    for y in range(NY):
        for x in range(NX):
            for c in range(2):
                source = (((y + dy) % NY) * NX + (x + dx) % NX) * 2 + (c ^ dc)
                pairs.append((source, (y * NX + x) * 2 + c))
    return lax.ppermute(value, "term", pairs)


def body(
    hidden_states,
    lengths,
    block_list,
    cluster_ids,
    attn_weight,
    out_weight,
    up_weight,
    down_weight,
    head_weight,
    head_gain,
    vocab_weight,
    vocab_bias,
    centroids,
):
    devices = lax.axis_size("grp") * lax.axis_size("term")
    passages = lengths.shape[0]

    side = 2 * NX
    rows_of_chips = [[g * side + k for k in range(side)] for g in range(NY)]
    vocab = lax.all_gather(
        vocab_weight, "term", axis=0, tiled=True, axis_index_groups=rows_of_chips
    )
    def spread(payload):
        return [payload] + [shift(payload, d, 0, 0) for d in OFFSETS[1:]]

    payload, dense, rest = encode_lead(
        hidden_states, lengths, block_list, head_gain,
        attn_weight, out_weight, up_weight, down_weight, head_weight,
    )
    early = spread(payload)
    payload, routed = encode_tail(
        rest, lengths, cluster_ids, block_list, head_gain, dense,
        up_weight, down_weight, head_weight, devices,
    )
    late = spread(payload)
    recv = lax.all_to_all(routed, ("grp", "term"), split_axis=0, concat_axis=0, tiled=True)

    scored = score(early + late[:1], vocab, None)
    sent = score(late[1:], vocab, scored)
    pieces = []
    for dx, dc in PEERS:
        back = sent[PEERS.index(((NX - dx) % NX, dc))]
        pieces.append(back if (dx, dc) == (0, 0) else shift(back, 0, dx, dc))
    sparse = finish(vocab_bias, pieces)
    dense_part, slot_part = place(recv, centroids, passages)
    return (sparse, dense_part[None], slot_part[:, :CAP])


def solution(mesh):
    placed = (
        P(("grp", "term"), None),
        P(("grp", "term")),
        P(("grp", "term"), None),
        P(("grp", "term")),
        P(),
        P(),
        P(),
        P(),
        P(),
        P(),
        P("term", None),
        P("term"),
        P(("grp", "term"), None),
    )
    return jax.shard_map(
        body,
        mesh=mesh,
        in_specs=placed,
        out_specs=(P("grp", "term"), P(("grp", "term"), None, None), P(("grp", "term"), None)),
        check_vma=False,
    )
```

```python
import functools
import math

import jax
import jax.numpy as jnp
from jax import lax
from jax.experimental import pallas as pl
from jax.experimental.pallas import tpu as pltpu
from jax.sharding import PartitionSpec as P

HEAD = 64
BLOCK = 128
SEQ = 128
CL_DEV = 512
CAP = 16
NX = 4
NY = 4
FCH = 512
EXTRA = 16
META = 128
STEP = 256
GROUP = 4
PARTS = 2
OFFSETS = (0, 1, 3, 2)
ORDER_Y = (0, 2, 1, 3)
PEERS = tuple((dx, dc) for dx in OFFSETS for dc in (0, 1))
FILL = -1e30
F32 = jnp.float32
BF16 = jnp.bfloat16
I32 = jnp.int32
VMEM_BYTES = 62 * 1024 * 1024

TAIL = (
    -0.9999988675117493,
    -1.151123285293579,
    -0.4591154456138611,
    -0.05271419882774353,
    0.007333385292440653,
    -0.0003233428578823805,
    -0.00011446241842349991,
    2.508325815142598e-05,
    -1.6903979940252611e-06,
)


def vmem():
    return pl.BlockSpec(memory_space=pltpu.VMEM)


def smem():
    return pl.BlockSpec(memory_space=pltpu.SMEM)


def hbm():
    return pl.BlockSpec(memory_space=pltpu.HBM)


def gelu(x):
    mag = jnp.abs(x)
    power = jnp.full_like(mag, TAIL[-1])
    for coefficient in TAIL[-2::-1]:
        power = power * mag + coefficient
    return jnp.maximum(x, 0.0) - mag * jnp.exp2(power)


def normalize(values):
    width = values.shape[-1]
    center = values - jnp.sum(values, axis=-1, keepdims=True) * (1.0 / width)
    spread = jnp.sum(center * center, axis=-1, keepdims=True) * (1.0 / width)
    return center * lax.rsqrt(spread + 1e-06)


def feed(
    offset, lengths_ref, lists_ref, gain_ref, send_ref, first, up_v, down_v, head_v, wide, acc, waits
):
    rows, width = first.shape
    passages = rows // SEQ
    chunks = up_v.shape[0]
    half = chunks // 2

    def up(c):
        return jnp.dot(first[...], up_v[c], preferred_element_type=F32)

    for part, ready in zip((0, half), waits):
        for d in ready:
            d.wait()
        current = up(part)
        for c in range(part, part + half):
            following = up(c + 1) if c + 1 < part + half else None
            wide[:, c * FCH : (c + 1) * FCH] = gelu(current).astype(BF16)
            current = following
    second = first[...].astype(F32) + jnp.dot(
        wide[...], down_v[...], preferred_element_type=F32
    )
    layer_out = normalize(second).astype(BF16)
    first[...] = layer_out
    middle = gelu(jnp.dot(layer_out, head_v[...], preferred_element_type=F32))
    acc[...] = normalize(middle) * gain_ref[...].reshape(1, width)

    row = lax.broadcasted_iota(I32, (SEQ, 1), 0)
    slots = lists_ref.shape[1]
    block_id = lax.broadcasted_iota(I32, (BLOCK, slots), 0)
    send_ref[rows:, :] = jnp.zeros((EXTRA, width), BF16)
    for p in range(passages):
        base = p * SEQ
        send_ref[base : base + SEQ, :] = jnp.where(
            row < lengths_ref[offset + p], acc[base : base + SEQ, :], acc[base : base + 1, :]
        ).astype(BF16)
        hit = (lists_ref[offset + p : offset + p + 1, :] == block_id).astype(F32).astype(BF16)
        count = lax.dot_general(
            jnp.ones((8, slots), BF16), hit, (((1,), (1,)), ((), ())), preferred_element_type=F32
        )
        send_ref[rows + p : rows + p + 1, 0:BLOCK] = count[0:1, :].astype(BF16)


def feed_moves(up_hbm, down_hbm, head_hbm, up_v, down_v, head_v):
    moves = [
        (up_hbm.at[:, pl.ds(c * FCH, FCH)], up_v.at[c]) for c in range(up_v.shape[0])
    ]
    return moves + [(down_hbm, down_v), (head_hbm, head_v)]


def feed_scratch(rows, width, ff):
    return [
        pltpu.VMEM((rows, width), BF16),
        pltpu.VMEM((ff // FCH, width, FCH), BF16),
        pltpu.VMEM((ff, width), BF16),
        pltpu.VMEM((width, width), BF16),
        pltpu.VMEM((rows, ff), BF16),
        pltpu.VMEM((rows, width), F32),
    ]


def start(moves, sems):
    dma = [pltpu.make_async_copy(s, d, sems.at[i]) for i, (s, d) in enumerate(moves)]
    for d in dma:
        d.start()
    return dma


def lead_kernel(
    lengths_ref, hidden_hbm, lists_ref, gain_ref, attn_hbm, out_hbm, up_hbm, down_hbm, head_hbm,
    send_ref, dense_ref, rest_ref,
    hidden, attn_v, out_v, joined, context, first, up_v, down_v, head_v, wide, acc, sems,
):
    rows, width = hidden.shape
    passages = rows // SEQ
    lead = first.shape[0] // SEQ
    pairs = width // 128
    moves = [(hidden_hbm, hidden)]
    for k in range(3):
        moves.append((attn_hbm.at[:, pl.ds(k * width, width)], attn_v.at[k]))
    moves.append((out_hbm, out_v))
    dma = start(
        moves + feed_moves(up_hbm, down_hbm, head_hbm, up_v, down_v, head_v), sems
    )
    dma[0].wait()
    dma[1].wait()
    for k in range(3):
        if k == 1:
            for d in dma[2:5]:
                d.wait()
        joined[:, k * width : (k + 1) * width] = jnp.dot(
            hidden[...], attn_v[k], preferred_element_type=F32
        ).astype(BF16)

    low = lax.broadcasted_iota(I32, (SEQ, 128), 1) < HEAD
    lane = lax.broadcasted_iota(I32, (2 * SEQ, 128), 1)
    scale = math.log2(math.e) / math.sqrt(HEAD)
    for p in range(passages):
        at = slice(p * SEQ, (p + 1) * SEQ)
        length = lengths_ref[p]
        for h in range(pairs):
            q = joined[at, h * 128 : (h + 1) * 128]
            k = joined[at, width + h * 128 : width + (h + 1) * 128]
            v = joined[at, 2 * width + h * 128 : 2 * width + (h + 1) * 128]
            zero = jnp.zeros_like(q)
            both = jnp.concatenate([jnp.where(low, q, zero), jnp.where(low, zero, q)], axis=0)
            s = lax.dot_general(both, k, (((1,), (1,)), ((), ())), preferred_element_type=F32)
            s = jnp.where(lane < length, s, FILL)
            top = jnp.max(s, axis=-1, keepdims=True)
            e = jnp.exp2((s - top) * scale)
            total = 1.0 / jnp.sum(e, axis=-1, keepdims=True)
            o = jnp.dot(e.astype(BF16), v, preferred_element_type=F32)
            mix = jnp.where(low, o[:SEQ] * total[:SEQ], o[SEQ:] * total[SEQ:])
            context[at, h * 128 : (h + 1) * 128] = mix.astype(BF16)

    for p in range(passages):
        at = slice(p * SEQ, (p + 1) * SEQ)
        mixed = hidden[at, :].astype(F32) + jnp.dot(
            context[at, :], out_v[...], preferred_element_type=F32
        )
        into, k = (first, p) if p < lead else (rest_ref, p - lead)
        into[k * SEQ : (k + 1) * SEQ, :] = normalize(mixed).astype(BF16)

    feed(
        0, lengths_ref, lists_ref, gain_ref, send_ref, first, up_v, down_v, head_v, wide, acc,
        (dma[5:], ()),
    )
    for p in range(lead):
        dense_ref[p : p + 1, :] = first[p * SEQ : p * SEQ + 1, :].astype(F32)


def encode_lead(hidden, lengths, block_list, gain, attn_w, out_w, up_w, down_w, head_w):
    rows, width = hidden.shape
    part = rows // PARTS
    ff = up_w.shape[1]
    return pl.pallas_call(
        lead_kernel,
        out_shape=(
            jax.ShapeDtypeStruct((part + EXTRA, width), BF16),
            jax.ShapeDtypeStruct((8, width), F32),
            jax.ShapeDtypeStruct((rows - part, width), BF16),
        ),
        in_specs=[smem(), hbm(), vmem(), vmem()] + [hbm()] * 5,
        out_specs=(vmem(), vmem(), vmem()),
        scratch_shapes=[
            pltpu.VMEM((rows, width), BF16),
            pltpu.VMEM((3, width, width), BF16),
            pltpu.VMEM((width, width), BF16),
            pltpu.VMEM((rows, 3 * width), BF16),
            pltpu.VMEM((rows, width), BF16),
        ] + feed_scratch(part, width, ff) + [pltpu.SemaphoreType.DMA((7 + ff // FCH,))],
        compiler_params=pltpu.CompilerParams(vmem_limit_bytes=VMEM_BYTES),
        cost_estimate=pl.CostEstimate(
            flops=2 * rows * width * 4 * width, transcendentals=0, bytes_accessed=8 * width * width
        ),
        name="lead",
    )(lengths, hidden, block_list, gain, attn_w, out_w, up_w, down_w, head_w)


def tail_kernel(
    lengths_ref, clusters_ref, rest_hbm, lists_ref, gain_ref, dense_ref, up_hbm, down_hbm, head_hbm,
    send_ref, route_ref,
    first, up_v, down_v, head_v, wide, acc, sems,
):
    rows, width = first.shape
    lead = clusters_ref.shape[0] - rows // SEQ
    half = up_v.shape[0] // 2
    dma = start(
        [(rest_hbm, first)] + feed_moves(up_hbm, down_hbm, head_hbm, up_v, down_v, head_v), sems
    )
    feed(
        lead, lengths_ref, lists_ref, gain_ref, send_ref, first, up_v, down_v, head_v, wide, acc,
        (dma[: 1 + half], dma[1 + half :]),
    )
    dense = [dense_ref[p : p + 1, :] for p in range(lead)]
    dense += [first[p : p + 1, :].astype(F32) for p in range(0, rows, SEQ)]

    devices = route_ref.shape[0]
    pieces = width // META
    row = lax.broadcasted_iota(I32, (devices, 1), 0)
    lane = lax.broadcasted_iota(I32, (devices, META), 1)
    term = lax.axis_index("term").astype(I32)
    device = lax.axis_index("grp").astype(I32) * lax.axis_size("term") + term
    parts = [jnp.zeros((devices, META), F32) for _ in range(pieces)]
    meta = jnp.zeros((devices, META), I32)
    for p, values in enumerate(dense):
        cluster = clusters_ref[p]
        owner = lax.div(cluster, CL_DEV)
        mine = row == owner
        for k in range(pieces):
            parts[k] = jnp.where(mine, values[:, k * META : (k + 1) * META], parts[k])
        word = jnp.where(lane == 0, 1, 0)
        word = jnp.where(lane == 1, device, word)
        word = jnp.where(lane == 2, p, word)
        word = jnp.where(lane == 3, cluster - owner * CL_DEV, word)
        meta = jnp.where(mine, word, meta)
    for k in range(pieces):
        route_ref[:, k, :] = parts[k]
    route_ref[:, pieces, :] = meta.astype(F32)
    route_ref[:, pieces + 1, :] = jnp.zeros((devices, META), F32)


def encode_tail(rest, lengths, clusters, block_list, gain, dense, up_w, down_w, head_w, devices):
    rows, width = rest.shape
    ff = up_w.shape[1]
    return pl.pallas_call(
        tail_kernel,
        out_shape=(
            jax.ShapeDtypeStruct((rows + EXTRA, width), BF16),
            jax.ShapeDtypeStruct((devices, 8, META), F32),
        ),
        in_specs=[smem(), smem(), hbm(), vmem(), vmem(), vmem(), hbm(), hbm(), hbm()],
        out_specs=(vmem(), vmem()),
        scratch_shapes=feed_scratch(rows, width, ff)
        + [pltpu.SemaphoreType.DMA((3 + ff // FCH,))],
        compiler_params=pltpu.CompilerParams(vmem_limit_bytes=VMEM_BYTES),
        cost_estimate=pl.CostEstimate(flops=1, transcendentals=0, bytes_accessed=1),
        name="tail",
    )(lengths, clusters, rest, block_list, gain, dense, up_w, down_w, head_w)


def here():
    term = lax.axis_index("term").astype(I32)
    chip = lax.div(term, 2)
    return lax.div(chip, NX), lax.rem(chip, NX), lax.rem(term, 2)


def place_kernel(passages, recv_ref, cent_ref, dense_ref, slot_ref):
    devices = recv_ref.shape[0]
    width = dense_ref.shape[1]
    pieces = width // META
    words = recv_ref[:, pieces, :]
    high = jnp.floor(words * (1.0 / 256.0))
    meta = words.astype(BF16)
    source = lax.broadcasted_iota(I32, (devices, devices), 0)
    other = lax.broadcasted_iota(I32, (devices, devices), 1)
    before = (other < source).astype(F32).astype(BF16)
    valid = words[:, 0:1]
    rank = jnp.dot(before, meta, preferred_element_type=F32)[:, 0:1]
    slot = lax.broadcasted_iota(I32, (devices, META), 1).astype(F32)
    chosen = ((rank == slot) & (valid > 0.5)).astype(F32).astype(BF16)
    over = (((0,), (0,)), ((), ()))

    def pick(values):
        return lax.dot_general(
            chosen, values.astype(BF16), over, preferred_element_type=F32
        )[:CAP]

    small = pick(words - high * 256.0)
    large = pick(high)
    filled = small[:, 0:1] > 0.5
    local = (small + large * 256.0)[:, 3:4]
    ids = lax.broadcasted_iota(I32, (CAP, cent_ref.shape[0]), 1).astype(F32)
    lookup = ((ids == local) & filled).astype(F32).astype(BF16)
    center = jnp.dot(lookup, cent_ref[...], preferred_element_type=F32)
    for k in range(pieces):
        at = slice(k * META, (k + 1) * META)
        dense_ref[:, at] = jnp.where(
            filled, pick(recv_ref[:, k, :]) - center[:, at], 0.0
        ).astype(BF16)
    names = lax.dot_general(meta, chosen, over, preferred_element_type=F32)
    ident = names[1:2, :] * passages + names[2:3, :]
    slot_ref[...] = jnp.where(names[0:1, :] > 0.5, ident, -1.0).astype(I32)


def place(recv, centroids, passages):
    width = centroids.shape[1]
    return pl.pallas_call(
        functools.partial(place_kernel, passages),
        out_shape=(
            jax.ShapeDtypeStruct((CAP, width), BF16),
            jax.ShapeDtypeStruct((1, META), I32),
        ),
        in_specs=[vmem(), vmem()],
        out_specs=(vmem(), vmem()),
        name="place",
    )(recv, centroids)


def score_kernel(tokens, vocab_hbm, res, listed, tok_v, side_v, w_v, tok_sem, side_sem, w_sem):
    groups = len(tokens)
    rows = tok_v.shape[0] // groups
    passages = rows // SEQ
    shards, terms = w_v.shape[:2]
    per_device = terms // BLOCK
    tok_dma, side_dma = [], []
    for g, t in enumerate(tokens):
        tok_dma.append(
            pltpu.make_async_copy(
                t.at[pl.ds(0, rows), :], tok_v.at[pl.ds(g * rows, rows), :], tok_sem.at[g]
            )
        )
        side_dma.append(
            pltpu.make_async_copy(
                t.at[pl.ds(rows, EXTRA), pl.ds(0, BLOCK)], side_v.at[g], side_sem.at[g]
            )
        )

    def shard(s):
        at = pl.ds(s * terms if isinstance(s, int) else pl.multiple_of(s * terms, terms), terms)
        return pltpu.make_async_copy(vocab_hbm.at[at, :], w_v.at[s], w_sem.at[s])

    for d in side_dma + tok_dma:
        d.start()
    for s in range(shards):
        shard(s).start()
    y, _, _ = here()
    source = lax.broadcasted_iota(I32, (BLOCK, terms), 0)
    target = lax.div(lax.broadcasted_iota(I32, (BLOCK, terms), 1), BLOCK)
    for d in side_dma:
        d.wait()
    side = jnp.concatenate([side_v[g].astype(F32)[:passages] for g in range(groups)], axis=0)
    side = side.astype(BF16)

    for s in range(shards):
        spread = (source == target + (y * shards + s) * per_device).astype(F32).astype(BF16)
        listed[s] = jnp.dot(side, spread, preferred_element_type=F32)

    for d in tok_dma:
        d.wait()

    @pl.loop(0, shards // GROUP)
    def _(step):
        for k in range(GROUP):
            shard(step * GROUP + k).wait()
        for k in range(GROUP):
            s = step * GROUP + k
            for n in range(terms // STEP):
                at = slice(n * STEP, (n + 1) * STEP)
                logits = lax.dot_general(
                    tok_v[...], w_v[s, at, :], (((1,), (1,)), ((), ())),
                    preferred_element_type=F32,
                )
                best = jnp.max(logits.reshape(groups * passages, SEQ, STEP), axis=1)
                res[s, :, at] = jnp.where(listed[s, :, at] > 0.5, best, FILL)


def score(tokens, vocab, earlier):
    groups = len(tokens)
    rows, width = tokens[0].shape
    rows -= EXTRA
    shards = 2 * NX
    terms = vocab.shape[0] // shards
    part = groups * rows // SEQ
    last = earlier is not None

    def kernel(*refs):
        toks, voc, refs = refs[:groups], refs[groups], refs[groups + 1 :]
        if not last:
            score_kernel(toks, voc, *refs)
            return
        before, outs, res = refs[0], refs[1 : 1 + shards], refs[1 + shards]
        score_kernel(toks, voc, *refs[1 + shards :])
        _, x, core = here()
        for k, (dx, dc) in enumerate(PEERS):
            spot = lax.rem(x + dx, NX) * 2 + lax.rem(core + dc, 2)
            outs[k][:done, :] = before[spot]
            outs[k][done:, :] = res[spot]

    flops = 2 * groups * rows * width * terms * shards
    whole = jax.ShapeDtypeStruct((shards, part, terms), F32)
    done = earlier.shape[1] if last else 0
    piece = jax.ShapeDtypeStruct((done + part, terms), F32)
    return pl.pallas_call(
        kernel,
        out_shape=(piece,) * shards if last else whole,
        in_specs=[hbm()] * (groups + 1) + [vmem()] * last,
        out_specs=(vmem(),) * shards if last else vmem(),
        scratch_shapes=[pltpu.VMEM(whole.shape, F32)] * (1 + last) + [
            pltpu.VMEM((groups * rows, width), BF16),
            pltpu.VMEM((groups, EXTRA, BLOCK), BF16),
            pltpu.VMEM((shards, terms, width), BF16),
            pltpu.SemaphoreType.DMA((groups,)),
            pltpu.SemaphoreType.DMA((groups,)),
            pltpu.SemaphoreType.DMA((shards,)),
        ],
        compiler_params=pltpu.CompilerParams(vmem_limit_bytes=VMEM_BYTES),
        cost_estimate=pl.CostEstimate(
            flops=flops, transcendentals=0, bytes_accessed=shards * terms * width * 2
        ),
        name="score",
    )(*tokens, vocab, *((earlier,) if last else ()))


def finish_kernel(bias_ref, *refs):
    pieces, (out_ref, best) = refs[: len(PEERS)], refs[len(PEERS) :]
    y, x, core = here()
    bias = bias_ref[...].astype(F32).reshape(1, -1)
    share = pieces[0].shape[0] // PARTS
    few = share // NY
    for k in range(0, len(PEERS), 2):
        dx = PEERS[k][0]
        for g, dy in enumerate(ORDER_Y):
            same, other = (
                [pieces[k + c][h * share + g * few : h * share + (g + 1) * few, :] for h in range(PARTS)]
                for c in range(2)
            )
            tile = jnp.where(
                core == 0,
                jnp.concatenate(same + other, axis=0),
                jnp.concatenate(other + same, axis=0),
            )
            spot = lax.rem(y + dy, NY) * NX + lax.rem(x + dx, NX)
            best[pl.ds(pl.multiple_of(spot * 8, 8), 8), :] = tile
    out_ref[...] = jnp.log1p(jnp.maximum(best[...] + bias, 0.0)).astype(BF16)


def finish(bias, pieces):
    terms = bias.shape[0]
    rows = NX * NY * 8
    return pl.pallas_call(
        finish_kernel,
        out_shape=jax.ShapeDtypeStruct((rows, terms), BF16),
        in_specs=[vmem()] * (1 + len(pieces)),
        out_specs=vmem(),
        scratch_shapes=[pltpu.VMEM((rows, terms), F32)],
        name="finish",
    )(bias, *pieces)


def shift(value, dy, dx, dc):
    pairs = []
    for y in range(NY):
        for x in range(NX):
            for c in range(2):
                source = (((y + dy) % NY) * NX + (x + dx) % NX) * 2 + (c ^ dc)
                pairs.append((source, (y * NX + x) * 2 + c))
    return lax.ppermute(value, "term", pairs)


def body(
    hidden_states,
    lengths,
    block_list,
    cluster_ids,
    attn_weight,
    out_weight,
    up_weight,
    down_weight,
    head_weight,
    head_gain,
    vocab_weight,
    vocab_bias,
    centroids,
):
    devices = lax.axis_size("grp") * lax.axis_size("term")
    passages = lengths.shape[0]

    side = 2 * NX
    rows_of_chips = [[g * side + k for k in range(side)] for g in range(NY)]
    vocab = lax.all_gather(
        vocab_weight, "term", axis=0, tiled=True, axis_index_groups=rows_of_chips
    )
    def spread(payload):
        return [payload] + [shift(payload, d, 0, 0) for d in ORDER_Y[1:]]

    payload, dense, rest = encode_lead(
        hidden_states, lengths, block_list, head_gain,
        attn_weight, out_weight, up_weight, down_weight, head_weight,
    )
    early = spread(payload)
    payload, routed = encode_tail(
        rest, lengths, cluster_ids, block_list, head_gain, dense,
        up_weight, down_weight, head_weight, devices,
    )
    late = spread(payload)
    recv = lax.all_to_all(routed, ("grp", "term"), split_axis=0, concat_axis=0, tiled=True)

    scored = score(early + late[:1], vocab, None)
    sent = score(late[1:], vocab, scored)
    pieces = []
    for dx, dc in PEERS:
        back = sent[PEERS.index(((NX - dx) % NX, dc))]
        pieces.append(back if (dx, dc) == (0, 0) else shift(back, 0, dx, dc))
    sparse = finish(vocab_bias, pieces)
    dense_part, slot_part = place(recv, centroids, passages)
    return (sparse, dense_part[None], slot_part[:, :CAP])


def solution(mesh):
    placed = (
        P(("grp", "term"), None),
        P(("grp", "term")),
        P(("grp", "term"), None),
        P(("grp", "term")),
        P(),
        P(),
        P(),
        P(),
        P(),
        P(),
        P("term", None),
        P("term"),
        P(("grp", "term"), None),
    )
    return jax.shard_map(
        body,
        mesh=mesh,
        in_specs=placed,
        out_specs=(P("grp", "term"), P(("grp", "term"), None, None), P(("grp", "term"), None)),
        check_vma=False,
    )
```
